512 devices in a mesh: conv: 8 (over y, core), seq: 8 (over z_lo), tensor: 8 (over z_hi, x).
Axes of the slice: x: 4, y: 4, z: 16 (z_hi: 2, z_lo: 8; z = z_hi * 8 + z_lo), core: 2. Of those that a mesh axis runs over, the one named last changes fastest.
Arguments:
- queries: bfloat16 [8, 1024, 4096], P('conv', 'seq', 'tensor'), may hold values from -6 to 6
- keys: bfloat16 [16, 1664, 1024], P('conv', ('seq', 'tensor')), may hold values from -6 to 6
- values: bfloat16 [16, 1664, 1024], P('conv', ('seq', 'tensor')), may hold values from -18 to 18
- q_gain: float32 [128], replicated, may hold values from 0.9 to 2.2
- k_gain: float32 [128], replicated, may hold values from 0.9 to 2.2
- gate: float32 [1], replicated, may hold values from 0.4 to 1.6
- tile_count: int32 [8], replicated, may hold values from 1 to 2, as said below
- tile_owner: int32 [8, 2], replicated, may hold values from -1 to 7, as said below
- visible: int32 [8, 1024], replicated, may hold values from 0 to 2, as said below
- d_out: bfloat16 [8, 1024, 4096], P('conv', 'seq', 'tensor'), may hold values from -12 to 12
Outputs:
- attended: bfloat16 [8, 1024, 4096], P('conv', 'seq', 'tensor')
- d_queries: bfloat16 [8, 1024, 4096], P('conv', 'seq', 'tensor')
- d_keys: bfloat16 [16, 1664, 1024], P('conv', ('seq', 'tensor'))
- d_values: bfloat16 [16, 1664, 1024], P('conv', ('seq', 'tensor'))
The draws below stay inside these ranges and needn't reach their ends.
Inputs may be any that keep to these rules, and one draw needn't show every extreme that they name: `tile_count`: some conversation has 2 tiles. `tile_owner`: entries with t at or past the conversation's count are -1. The tiles of one conversation have different owners, no two tiles share a slot, and some conv index holds 2 tiles. `visible`: never falls along a conversation's text; it is 0 at the first token and 2 at the last.
All inputs are finite; a program needn't handle non-finite values.
Results may differ from the reference program's by a relative error of at most 0.02.
Values may be sent and summed in bfloat16 or wider, within the bound.
No kernel may reach another device: no remote copies, remote signals or barrier semaphores. Data moves between devices by JAX's collectives and lax.ppermute only.
A program may use at most 64 MiB of HBM per device.

```python
import math
import jax
import jax.numpy as jnp
from jax import lax

HD = 128
QHEADS = 32
KVHEADS = 8
MAXT = 2
TILE = 1601
TOK_SEQ = 128
GROUP = 4
TILE_PAD = 1664
LENGTH = 1024
N_CONV = 8
N_SEQ = 8


def tile_plan(key):
    plan_key = jax.random.fold_in(key, 11)
    key_rows, key_cols, key_names, key_full, key_counts = jax.random.split(plan_key, 5)
    row_shift = jax.random.permutation(key_rows, N_CONV)
    col_shift = jax.random.permutation(key_cols, N_CONV)[:MAXT]
    relabel = jax.random.permutation(key_names, N_CONV)
    owners = relabel[(row_shift[:, None] + col_shift[None, :]) % N_CONV]
    full_owner = jax.random.randint(key_full, (), 0, N_CONV)
    tile_ids = jnp.arange(MAXT, dtype=jnp.int32)
    needed = jnp.max(jnp.where(owners == full_owner, tile_ids[None, :] + 1, 0), axis=1)
    counts = jnp.maximum(jax.random.randint(key_counts, (N_CONV,), 1, MAXT + 1), needed)
    owner_table = jnp.where(tile_ids[None, :] < counts[:, None], owners, -1)
    return (counts.astype(jnp.int32), owner_table.astype(jnp.int32))


def draw_tile_count(key, part):
    return tile_plan(key)[0]


def draw_tile_owner(key, part):
    return tile_plan(key)[1]


def draw_visible(key, part):
    thresholds = jax.random.randint(jax.random.fold_in(key, 23), (N_CONV, MAXT), 1, LENGTH)
    positions = jnp.arange(LENGTH, dtype=jnp.int32)
    return jnp.sum(thresholds[:, :, None] <= positions[None, None, :], axis=1).astype(jnp.int32)


def level_of(rng, dims, cuts, smallest, largest):
    loudness = 1.0
    for position, blocks in cuts:
        steps = jax.random.uniform(jax.random.fold_in(jax.random.fold_in(rng, 6), position), (blocks,), jnp.float32, smallest / len(cuts), largest / len(cuts))
        loudness = loudness * jnp.repeat(jnp.exp(steps), dims[position] // blocks).reshape((-1,) + (1,) * (len(dims) - 1 - position))
    return loudness


def centred(key, shape, deviation, limit, pieces=(), kind=jnp.bfloat16):
    values = jax.random.normal(key, shape, jnp.float32) * deviation
    if len(pieces) > 0:
        values = level_of(key, shape, pieces, -0.22, 0.18) * values
    return jnp.clip(values, min=-limit, max=limit).astype(kind)


def setup_inputs(seed: int = 0) -> dict:
    seeds = jax.random.split(jax.random.key(seed), 11)
    queries = centred(seeds[0], (N_CONV, LENGTH, QHEADS * HD), 1.0, 6.0, ((0, 8), (1, 8), (2, 8)))
    keys = centred(seeds[1], (N_CONV * MAXT, TILE_PAD, KVHEADS * HD), 1.0, 6.0, ((0, 8), (1, 64)))
    values = centred(seeds[2], (N_CONV * MAXT, TILE_PAD, KVHEADS * HD), 3.0, 18.0, ((0, 8), (1, 64)))
    q_gain = jnp.clip(jnp.exp(jax.random.uniform(seeds[3], (HD,), jnp.float32, math.log(0.9), math.log(2.2))), 0.9, 2.2)
    k_gain = jnp.clip(jnp.exp(jax.random.uniform(seeds[4], (HD,), jnp.float32, math.log(0.9), math.log(2.2))), 0.9, 2.2)
    gate = jnp.clip(jax.random.uniform(seeds[5], (1,), jnp.float32, 0.4, 1.6), 0.4, 1.6)
    tile_count = draw_tile_count(jax.random.fold_in(seeds[10], 71), 0)
    tile_owner = draw_tile_owner(jax.random.fold_in(seeds[10], 71), 0)
    visible = draw_visible(jax.random.fold_in(seeds[10], 71), 0)
    d_out = centred(seeds[9], (N_CONV, LENGTH, QHEADS * HD), 2.0, 12.0, ((0, 8), (1, 8), (2, 8)))
    return dict(queries=queries, keys=keys, values=values, q_gain=q_gain, k_gain=k_gain, gate=gate, tile_count=tile_count, tile_owner=tile_owner, visible=visible, d_out=d_out)


EPSILON = 1e-05

def head_norm(inputs, norm_gain):
    mean_square = lax.optimization_barrier(jnp.mean(inputs * inputs, axis=-1, keepdims=True))
    return inputs * lax.rsqrt(mean_square + EPSILON) * norm_gain

def rounded(inputs):
    return lax.optimization_barrier(inputs.astype(jnp.bfloat16)).astype(jnp.float32)

def reference(queries, keys, values, q_gain, k_gain, gate, tile_count, tile_owner, visible, d_out):
    score_scale = 1.0 / math.sqrt(HD)
    gate_value = jnp.tanh(gate[0])
    slots_all = N_CONV * MAXT
    key_raw = keys.astype(jnp.float32).reshape(slots_all, TILE_PAD, KVHEADS, HD)
    key_normed, key_back = jax.vjp(lambda inputs: head_norm(inputs, k_gain), key_raw)
    key_halfprec = key_normed.astype(jnp.bfloat16)
    value_all = values.reshape(slots_all, TILE_PAD, KVHEADS, HD)
    tile_ids = jnp.arange(MAXT, dtype=jnp.int32)
    row_ids = jnp.arange(TILE_PAD, dtype=jnp.int32)
    valid = tile_owner >= 0
    slot_index = jnp.where(valid, tile_owner * MAXT + tile_ids[None, :], 0).astype(jnp.int32)
    key_tile_ids = jnp.repeat(tile_ids, TILE_PAD)
    key_row_ids = jnp.tile(row_ids, MAXT)

    def one_conversation(conversation):
        chosen = slot_index[conversation]
        present = valid[conversation]
        tile_keys = jnp.where(present[:, None, None, None], key_halfprec[chosen], jnp.zeros((), jnp.bfloat16))
        tile_values = jnp.where(present[:, None, None, None], value_all[chosen], jnp.zeros((), jnp.bfloat16))
        flat_keys = tile_keys.reshape(MAXT * TILE_PAD, KVHEADS, HD).astype(jnp.float32)
        flat_values = tile_values.reshape(MAXT * TILE_PAD, KVHEADS, HD).astype(jnp.float32)
        seen_tiles = jnp.minimum(visible[conversation], tile_count[conversation])
        query_blocks = queries[conversation].astype(jnp.float32).reshape(N_SEQ, TOK_SEQ, QHEADS, HD)
        grad_blocks = d_out[conversation].astype(jnp.float32).reshape(N_SEQ, TOK_SEQ, KVHEADS, GROUP, HD)
        seen_blocks = seen_tiles.reshape(N_SEQ, TOK_SEQ)

        def one_block(carry, inputs):
            key_sum, value_sum = carry
            query_raw, cotangent, seen_here = inputs
            query_normed, query_back = jax.vjp(lambda vector: head_norm(vector, q_gain), query_raw)
            query_bf = rounded(query_normed).reshape(TOK_SEQ, KVHEADS, GROUP, HD)
            visible_keys = (key_tile_ids[None, :] < seen_here[:, None]) & (key_row_ids[None, :] < TILE)
            scores = jnp.einsum('pkgd,rkd->kgpr', query_bf, flat_keys) * score_scale
            weights = jnp.where(visible_keys[None, None], jnp.exp(scores), 0.0)
            weight_sum = lax.optimization_barrier(jnp.sum(weights, axis=-1))
            weighted = jnp.einsum('kgpr,rkd->pkgd', rounded(weights), flat_values)
            safe_sum = jnp.where(weight_sum > 0, weight_sum, 1.0)
            context = weighted / jnp.transpose(safe_sum, (2, 0, 1))[..., None]
            attended = (gate_value * context).astype(jnp.bfloat16).reshape(TOK_SEQ, QHEADS * HD)
            grad_ctx = rounded(gate_value * cotangent)
            row_delta = jnp.transpose(lax.optimization_barrier(jnp.sum(grad_ctx * context, axis=-1)), (1, 2, 0))
            probability = weights / safe_sum[..., None]
            grad_prob = jnp.einsum('pkgd,rkd->kgpr', grad_ctx, flat_values)
            grad_score = rounded(probability * (grad_prob - row_delta[..., None]))
            grad_query = jnp.einsum('kgpr,rkd->pkgd', grad_score, flat_keys) * score_scale
            query_grad = query_back(grad_query.reshape(TOK_SEQ, QHEADS, HD))[0]
            query_grad = query_grad.astype(jnp.bfloat16).reshape(TOK_SEQ, QHEADS * HD)
            key_part = jnp.einsum('kgpr,pkgd->rkd', grad_score, query_bf) * score_scale
            value_part = jnp.einsum('kgpr,pkgd->rkd', rounded(probability), grad_ctx)
            key_sum = key_sum + rounded(key_part)
            value_sum = value_sum + rounded(value_part)
            return ((key_sum, value_sum), (attended, query_grad))
        zero_grads = jnp.zeros((MAXT * TILE_PAD, KVHEADS, HD), jnp.float32)
        (key_sum, value_sum), (attended, query_grad) = lax.scan(one_block, (zero_grads, zero_grads), (query_blocks, grad_blocks, seen_blocks))
        key_grad = key_sum.astype(jnp.bfloat16).reshape(MAXT, TILE_PAD, KVHEADS, HD)
        value_grad = value_sum.astype(jnp.bfloat16).reshape(MAXT, TILE_PAD, KVHEADS, HD)
        return (attended.reshape(LENGTH, QHEADS * HD), query_grad.reshape(LENGTH, QHEADS * HD), key_grad, value_grad)
    attended, d_queries, key_grad, value_grad = lax.map(one_conversation, jnp.arange(N_CONV, dtype=jnp.int32))
    target = jnp.where(valid, tile_owner * MAXT + tile_ids[None, :], slots_all).astype(jnp.int32).reshape(-1)
    positioned_keys = jnp.zeros((slots_all, TILE_PAD, KVHEADS, HD), jnp.float32)
    positioned_keys = positioned_keys.at[target].add(key_grad.reshape(slots_all, TILE_PAD, KVHEADS, HD).astype(jnp.float32), mode='drop')
    placed_values = jnp.zeros((slots_all, TILE_PAD, KVHEADS, HD), jnp.float32)
    placed_values = placed_values.at[target].add(value_grad.reshape(slots_all, TILE_PAD, KVHEADS, HD).astype(jnp.float32), mode='drop')
    d_keys = key_back(positioned_keys)[0].astype(jnp.bfloat16).reshape(slots_all, TILE_PAD, KVHEADS * HD)
    d_values = placed_values.astype(jnp.bfloat16).reshape(slots_all, TILE_PAD, KVHEADS * HD)
    return (attended, d_queries, d_keys, d_values)
```

```python
import math

import jax
import jax.numpy as jnp
from jax import lax
from jax.experimental import pallas as pl
from jax.experimental.pallas import tpu as pltpu
from jax.sharding import Mesh, PartitionSpec as P

HD = 128
TILE = 1601
ROWS = 26
HALF = 16
EPSILON = 1e-05
SCALE = 1.0 / math.sqrt(HD)
SCALE_LOG2 = SCALE / math.log(2.0)
F32 = jnp.float32
BF16 = jnp.bfloat16

Y, CORE, Z, N_O, N_C = 4, 2, 8, 8, 8
CHUNK = 256
MID = 1024


def dot(a, b):
    return jnp.dot(a, b, preferred_element_type=F32)


def call(kernel, outs, *args, smem=0, scratch=(), flops=0, limit=None):
    specs = [pl.BlockSpec(memory_space=pltpu.SMEM)] * smem
    specs += [pl.BlockSpec(memory_space=pltpu.VMEM)] * (len(args) - smem)
    size = sum(a.size * a.dtype.itemsize for a in args) + sum(o.size * o.dtype.itemsize for o in outs)
    return pl.pallas_call(
        kernel,
        out_shape=outs,
        in_specs=specs,
        out_specs=[pl.BlockSpec(memory_space=pltpu.VMEM)] * len(outs),
        scratch_shapes=list(scratch),
        cost_estimate=pl.CostEstimate(flops=flops, bytes_accessed=size, transcendentals=0),
        compiler_params=pltpu.CompilerParams(vmem_limit_bytes=limit),
    )(*args)


def shape(dims, dtype):
    return jax.ShapeDtypeStruct(dims, dtype)


def pack_queries(gate_ref, queries_ref, d_out_ref, gain_ref, out_ref):
    gain = gain_ref[...]
    gate = gate_ref[0]
    for g in range(4):
        lanes = slice(g * HD, (g + 1) * HD)
        x = queries_ref[0, :, lanes].astype(F32)
        mean_square = jnp.mean(x * x, axis=-1, keepdims=True)
        out_ref[0:128, lanes] = (x * lax.rsqrt(mean_square + EPSILON) * gain).astype(BF16)
    out_ref[128:256, :] = (gate * d_out_ref[0].astype(F32)).astype(BF16)


def pack_keys(keys_ref, values_ref, gain_ref, out_ref):
    gain = gain_ref[...]
    for n in range(2):
        for head in range(8):
            hhi, hx = divmod(head, 4)
            lanes = slice(head * HD, (head + 1) * HD)
            x = keys_ref[n, :, lanes].astype(F32)
            mean_square = jnp.mean(x * x, axis=-1, keepdims=True)
            normed = (x * lax.rsqrt(mean_square + EPSILON) * gain).astype(BF16)
            pad = jnp.zeros((2 * HALF - ROWS, HD), BF16)
            for kv, rows in ((0, normed), (1, values_ref[n, :, lanes])):
                for half in range(2):
                    at = (n * 2 + half) * 2 + kv
                    if half == 0:
                        out_ref[at, hx, hhi * HALF : (hhi + 1) * HALF, :] = rows[:HALF]
                    else:
                        out_ref[at, hx, hhi * HALF : (hhi + 1) * HALF, :] = jnp.concatenate([rows[HALF:], pad], axis=0)


def choose_tiles(owner_ref, got_ref, out_ref):
    for c in range(N_C):
        o = jnp.maximum(owner_ref[c], 0)
        chunk = got_ref[o]
        for hhi in range(2):
            out_ref[hhi, c] = chunk[:, hhi * HALF : (hhi + 1) * HALF, :].reshape(4 * HALF, HD)


def return_tiles(owner_ref, got_ref, out_ref):
    for o in range(N_O):
        found = jnp.int32(-1)
        for c in range(N_C):
            found = jnp.where(owner_ref[c] == o, c, found)
        at = jnp.maximum(found, 0)
        for hhi in range(2):
            chunk = jnp.where(found >= 0, got_ref[hhi, at].astype(F32), 0.0).astype(BF16)
            out_ref[o, :, hhi * HALF : (hhi + 1) * HALF, :] = chunk.reshape(4, HALF, HD)


def row_mask(half):
    position = lax.broadcasted_iota(jnp.int32, (MID, HD), 0)
    thi, s, tx, i = position >> 9, (position >> 6) & 7, (position >> 4) & 3, position & 15
    inside = half * HALF + i
    row = s * (8 * ROWS) + (thi * 4 + tx) * ROWS + inside
    return jnp.where((inside < ROWS) & (row < TILE), 1.0, 0.0).astype(F32)


def columns(rows):
    return jnp.concatenate([rows[:, g * HD : (g + 1) * HD].astype(F32).T for g in range(4)], axis=1)


def stacked(rows):
    return jnp.concatenate([rows[:, g * HD : (g + 1) * HD] for g in range(4)], axis=0)


def seen_row(ids_ref, count_ref, visible_ref, j):
    y, core, z = ids_ref[0], ids_ref[1], ids_ref[2]
    block = (((y - j) & 3) * 2 + core) ^ z
    seen = jnp.minimum(visible_ref[pl.ds(z * 8 + block, 1), :], count_ref[z])
    seen = jnp.where(seen > (y >> 1), 1.0, 0.0).astype(F32)
    return jnp.concatenate([seen] * 4, axis=1)


def masked_weights(keys_s, ok_s, q_t, rows):
    scores = dot(keys_s[rows, :], q_t)
    ok = ok_s[rows, :]
    return jnp.exp2(scores * SCALE_LOG2) * jnp.concatenate([ok] * 4, axis=1)


def load_pair(ids_ref, mine_ref, other_ref, keys_s, values_s, ok_s):
    core = ids_ref[1]

    @pl.when(core == 0)
    def _():
        keys_s[...] = mine_ref[...]
        values_s[...] = other_ref[...]

    @pl.when(core != 0)
    def _():
        keys_s[...] = other_ref[...]
        values_s[...] = mine_ref[...]

    ok_s[...] = row_mask(ids_ref[0] & 1)


def forward(ids_ref, count_ref, visible_ref, mine_ref, other_ref, q0, q1, q2, q3, acc_ref, sums_ref, keys_s, values_s, ok_s, turned_s, q_s):
    load_pair(ids_ref, mine_ref, other_ref, keys_s, values_s, ok_s)
    turned_s[...] = values_s[...].astype(F32).T.astype(BF16)
    for j, q in enumerate((q0, q1, q2, q3)):
        q_s[j] = q[...]

    def block(j, carry):
        q_t = columns(q_s[j, 0:128, :]).astype(BF16)
        o_t = columns(q_s[j, 128:256, :])
        total = jnp.zeros((1, 512), F32)
        acc = jnp.zeros((HD, 512), F32)
        for r in range(MID // CHUNK):
            rows = slice(r * CHUNK, (r + 1) * CHUNK)
            weights = masked_weights(keys_s, ok_s, q_t, rows)
            total = total + jnp.sum(weights, axis=0, keepdims=True)
            acc = acc + dot(turned_s[:, rows], weights.astype(BF16))
        seen = seen_row(ids_ref, count_ref, visible_ref, j)
        acc = acc * seen
        sums_ref[j] = jnp.concatenate([total * seen, jnp.sum(acc * o_t, axis=0, keepdims=True)], axis=0)
        acc_ref[j] = acc.astype(BF16)
        return carry

    lax.fori_loop(0, Y, block, 0)


def all_sums(s0, s1, s2, s3, j):
    both = s0[j] + s1[(j - 1) & 3] + s2[(j - 2) & 3] + s3[(j - 3) & 3]
    total = both[0:1]
    safe = jnp.where(total > 0, total, 1.0)
    return 1.0 / safe, both[1:2] / safe


def backward(
    ids_ref, count_ref, visible_ref, mine_ref, other_ref, q0, q1, q2, q3, s0, s1, s2, s3,
    dq_ref, keep_ref, send_ref, keys_s, values_s, ok_s, turned_s, q_s, dk_s, dv_s,
):
    load_pair(ids_ref, mine_ref, other_ref, keys_s, values_s, ok_s)
    turned_s[...] = keys_s[...].astype(F32).T.astype(BF16)
    dk_s[...] = jnp.zeros((MID, HD), F32)
    dv_s[...] = jnp.zeros((MID, HD), F32)
    for j, q in enumerate((q0, q1, q2, q3)):
        q_s[j] = q[...]

    def block(j, carry):
        q_t = columns(q_s[j, 0:128, :]).astype(BF16)
        o_t = columns(q_s[j, 128:256, :]).astype(BF16)
        q_rows = stacked(q_s[j, 0:128, :])
        o_rows = stacked(q_s[j, 128:256, :])
        inverse, delta = all_sums(s0, s1, s2, s3, j)
        inverse = inverse * seen_row(ids_ref, count_ref, visible_ref, j)
        dq = jnp.zeros((HD, 512), F32)
        for r in range(MID // CHUNK):
            rows = slice(r * CHUNK, (r + 1) * CHUNK)
            prob = masked_weights(keys_s, ok_s, q_t, rows) * inverse
            d_prob = dot(values_s[rows, :], o_t)
            d_score = (prob * (d_prob - delta)).astype(BF16)
            dk_s[rows, :] += dot(d_score, q_rows)
            dv_s[rows, :] += dot(prob.astype(BF16), o_rows)
            dq = dq + dot(turned_s[:, rows], d_score)
        dq_ref[j] = (dq * SCALE).astype(BF16)
        return carry

    lax.fori_loop(0, Y, block, 0)
    core = ids_ref[1]

    @pl.when(core == 0)
    def _():
        keep_ref[...] = dk_s[...] * SCALE
        send_ref[...] = dv_s[...].astype(BF16)

    @pl.when(core != 0)
    def _():
        keep_ref[...] = dv_s[...]
        send_ref[...] = (dk_s[...] * SCALE).astype(BF16)


def finish_attended(gate_ref, a0, a1, a2, a3, s0, s1, s2, s3, out_ref):
    inverse, _ = all_sums(s0, s1, s2, s3, 0)
    acc = a0[0].astype(F32) + a1[...].astype(F32) + a2[...].astype(F32) + a3[...].astype(F32)
    acc = acc * (inverse * gate_ref[0])
    for g in range(4):
        lanes = slice(g * HD, (g + 1) * HD)
        out_ref[:, lanes] = acc[:, lanes].T.astype(BF16)


def sum_queries(d0, d1, d2, d3, out_ref):
    dq = d0[0].astype(F32) + d1[...].astype(F32) + d2[...].astype(F32) + d3[...].astype(F32)
    for g in range(4):
        lanes = slice(g * HD, (g + 1) * HD)
        out_ref[:, lanes] = dq[:, lanes].T.astype(BF16)


def norm_back(x, d_normed, gain):
    mean_square = jnp.mean(x * x, axis=-1, keepdims=True)
    inverse = lax.rsqrt(mean_square + EPSILON)
    scaled = d_normed * gain
    dots = jnp.mean(x * scaled, axis=-1, keepdims=True)
    return inverse * scaled - x * (inverse * inverse * inverse * dots)


def finish_queries(queries_ref, dq_ref, gain_ref, out_ref):
    gain = gain_ref[...]
    for g in range(4):
        lanes = slice(g * HD, (g + 1) * HD)
        x = queries_ref[0, :, lanes].astype(F32)
        out_ref[0, :, lanes] = norm_back(x, dq_ref[:, lanes].astype(F32), gain).astype(BF16)


def finish_keys(keys_ref, got_ref, gain_ref, dk_ref, dv_ref):
    gain = gain_ref[...]
    for n in range(2):
        for head in range(8):
            hhi, hx = divmod(head, 4)
            lanes = slice(head * HD, (head + 1) * HD)
            for half, count in ((0, HALF), (1, ROWS - HALF)):
                at = (n * 2 + half) * 2
                rows = slice(half * HALF, half * HALF + count)
                piece = slice(hhi * HALF, hhi * HALF + count)
                dv_ref[n, rows, lanes] = got_ref[at + 1, hx, piece, :]
                x = keys_ref[n, rows, lanes].astype(F32)
                d_normed = got_ref[at, hx, piece, :].astype(F32)
                dk_ref[n, rows, lanes] = norm_back(x, d_normed, gain).astype(BF16)


def exchange(value, axes):
    return lax.all_to_all(value, axes, split_axis=0, concat_axis=0, tiled=True)


def rotated(value, k):
    return lax.ppermute(value, "y", [(i, (i + k) % Y) for i in range(Y)])


def swapped(value):
    return lax.ppermute(value, "core", [(0, 1), (1, 0)])


TO_PLANE = [(c * 8 + s, (s ^ c) * 8 + c) for c in range(8) for s in range(8)]
FROM_PLANE = [(b, a) for a, b in TO_PLANE]
PLANES = ("y", "core", "seq")


def shards(queries, keys, values, q_gain, k_gain, gate, tile_count, tile_owner, visible, d_out):
    y, core, z = lax.axis_index("y"), lax.axis_index("core"), lax.axis_index("seq")
    ids = jnp.stack([y, core, z]).astype(jnp.int32)
    gate_value = jnp.tanh(gate)
    q_gain = q_gain.reshape(1, HD)
    k_gain = k_gain.reshape(1, HD)
    owner = lax.dynamic_index_in_dim(tile_owner, y // 2, 1, keepdims=False)
    seen = visible.reshape(64, 128)

    (packed,) = call(pack_queries, [shape((256, 512), BF16)], gate_value, queries, d_out, q_gain, smem=1)
    q0 = lax.ppermute(packed, PLANES, TO_PLANE)
    (packed_kv,) = call(pack_keys, [shape((8, 4, 32, HD), BF16)], keys, values, k_gain)
    got = exchange(packed_kv.reshape(32, 32, HD), ("y", "core", "x"))
    (chosen,) = call(choose_tiles, [shape((2, 8, 64, HD), BF16)], owner, got.reshape(8, 4, 32, HD), smem=1)
    mine = exchange(chosen.reshape(16, 64, HD), ("zhi", "seq")).reshape(MID, HD)
    q1, q2, q3 = rotated(q0, 1), rotated(q0, 2), rotated(q0, 3)
    other = swapped(mine)

    common = [pltpu.VMEM((MID, HD), BF16), pltpu.VMEM((MID, HD), BF16), pltpu.VMEM((MID, HD), F32)]
    common += [pltpu.VMEM((HD, MID), BF16), pltpu.VMEM((Y, 256, 512), BF16)]
    acc, sums = call(
        forward,
        [shape((Y, HD, 512), BF16), shape((Y, 2, 512), F32)],
        ids, tile_count, seen, mine, other, q0, q1, q2, q3,
        smem=2, scratch=common, flops=2 * 2 * 2048 * MID * HD, limit=32 << 20,
    )
    s1, s2, s3 = rotated(sums, 1), rotated(sums, 2), rotated(sums, 3)
    a1, a2, a3 = rotated(acc[1], 3), rotated(acc[2], 2), rotated(acc[3], 1)
    dq, keep, send = call(
        backward,
        [shape((Y, HD, 512), BF16), shape((MID, HD), F32), shape((MID, HD), BF16)],
        ids, tile_count, seen, mine, other, q0, q1, q2, q3, sums, s1, s2, s3,
        smem=2, scratch=common + [pltpu.VMEM((MID, HD), F32)] * 2, flops=5 * 2 * 2048 * MID * HD, limit=32 << 20,
    )
    (attended,) = call(finish_attended, [shape((128, 512), BF16)], gate_value, acc, a1, a2, a3, sums, s1, s2, s3, smem=1)
    attended = lax.ppermute(attended, PLANES, FROM_PLANE)

    grads = (keep + swapped(send).astype(F32)).astype(BF16)
    back = exchange(grads.reshape(16, 64, HD), ("zhi", "seq"))
    d1, d2, d3 = rotated(dq[1], 3), rotated(dq[2], 2), rotated(dq[3], 1)
    (d_normed,) = call(sum_queries, [shape((128, 512), BF16)], dq, d1, d2, d3)
    d_normed = lax.ppermute(d_normed, PLANES, FROM_PLANE)
    (placed,) = call(return_tiles, [shape((8, 4, 32, HD), BF16)], owner, back.reshape(2, 8, 64, HD), smem=1)
    home = exchange(placed.reshape(32, 32, HD), ("y", "core", "x")).reshape(8, 4, 32, HD)
    d_keys, d_values = call(finish_keys, [shape(keys.shape, BF16), shape(values.shape, BF16)], keys, home, k_gain)
    (d_queries,) = call(finish_queries, [shape(queries.shape, BF16)], queries, d_normed, q_gain)
    return (attended[None], d_queries, d_keys, d_values)


def solution(mesh):
    parts = Mesh(mesh.devices.reshape(Y, CORE, Z, 2, 4), ("y", "core", "seq", "zhi", "x"))
    conv, tensor = ("y", "core"), ("zhi", "x")
    tokens = P(conv, "seq", tensor)
    rows = P(conv, ("seq", "zhi", "x"), None)
    in_specs = (tokens, rows, rows, P(), P(), P(), P(), P(), P(), tokens)
    out_specs = (tokens, tokens, rows, rows)
    return jax.shard_map(shards, mesh=parts, in_specs=in_specs, out_specs=out_specs, check_vma=False)
```

```python
import math

import jax
import jax.numpy as jnp
from jax import lax
from jax.experimental import pallas as pl
from jax.experimental.pallas import tpu as pltpu
from jax.sharding import Mesh, PartitionSpec as P

HD = 128
TILE = 1601
ROWS = 26
HALF = 16
EPSILON = 1e-05
SCALE = 1.0 / math.sqrt(HD)
SCALE_LOG2 = SCALE / math.log(2.0)
F32 = jnp.float32
BF16 = jnp.bfloat16

Y, CORE, Z, N_O, N_C = 4, 2, 8, 8, 8
PLANE_OF = (0, 7, 1, 6, 2, 5, 3, 4)
CONV_OF = tuple(PLANE_OF.index(z) for z in range(Z))
SHIFT = (0, 4, 1, 3, 2, 6, 5, 7)
CHUNK = 256
MID = 1024


def dot(a, b):
    return jnp.dot(a, b, preferred_element_type=F32)


def call(kernel, outs, *args, smem=0, scratch=(), flops=0, limit=8 << 20):
    specs = [pl.BlockSpec(memory_space=pltpu.SMEM)] * smem
    specs += [pl.BlockSpec(memory_space=pltpu.VMEM)] * (len(args) - smem)
    size = sum(a.size * a.dtype.itemsize for a in args) + sum(o.size * o.dtype.itemsize for o in outs)
    return pl.pallas_call(
        kernel,
        out_shape=outs,
        in_specs=specs,
        out_specs=[pl.BlockSpec(memory_space=pltpu.VMEM)] * len(outs),
        scratch_shapes=list(scratch),
        cost_estimate=pl.CostEstimate(flops=flops, bytes_accessed=size, transcendentals=0),
        compiler_params=pltpu.CompilerParams(vmem_limit_bytes=limit),
    )(*args)


def shape(dims, dtype):
    return jax.ShapeDtypeStruct(dims, dtype)


def pack_queries(gate_ref, queries_ref, d_out_ref, gain_ref, out_ref):
    gain = gain_ref[...]
    gate = gate_ref[0]
    for g in range(4):
        lanes = slice(g * HD, (g + 1) * HD)
        x = queries_ref[0, :, lanes].astype(F32)
        mean_square = jnp.mean(x * x, axis=-1, keepdims=True)
        out_ref[0:128, lanes] = (x * lax.rsqrt(mean_square + EPSILON) * gain).astype(BF16)
    out_ref[128:256, :] = (gate * d_out_ref[0].astype(F32)).astype(BF16)


def pack_keys(keys_ref, values_ref, gain_ref, out_ref):
    gain = gain_ref[...]
    for n in range(2):
        for head in range(8):
            hhi, hx = divmod(head, 4)
            lanes = slice(head * HD, (head + 1) * HD)
            x = keys_ref[n, :, lanes].astype(F32)
            mean_square = jnp.mean(x * x, axis=-1, keepdims=True)
            normed = (x * lax.rsqrt(mean_square + EPSILON) * gain).astype(BF16)
            pad = jnp.zeros((2 * HALF - ROWS, HD), BF16)
            for kv, rows in ((0, normed), (1, values_ref[n, :, lanes])):
                for half in range(2):
                    at = (n * 2 + half) * 2 + kv
                    if half == 0:
                        out_ref[at, hx, hhi * HALF : (hhi + 1) * HALF, :] = rows[:HALF]
                    else:
                        out_ref[at, hx, hhi * HALF : (hhi + 1) * HALF, :] = jnp.concatenate([rows[HALF:], pad], axis=0)


def choose_tiles(owner_ref, got_ref, out_ref):
    for z in range(Z):
        o = jnp.maximum(owner_ref[CONV_OF[z]], 0)
        chunk = got_ref[o]
        for hhi in range(2):
            out_ref[hhi, z] = chunk[:, hhi * HALF : (hhi + 1) * HALF, :].reshape(4 * HALF, HD)


def return_tiles(owner_ref, got_ref, out_ref):
    for o in range(N_O):
        found = jnp.int32(-1)
        for c in range(N_C):
            found = jnp.where(owner_ref[c] == o, PLANE_OF[c], found)
        at = jnp.maximum(found, 0)
        for hhi in range(2):
            chunk = jnp.where(found >= 0, got_ref[hhi, at].astype(F32), 0.0).astype(BF16)
            out_ref[o, :, hhi * HALF : (hhi + 1) * HALF, :] = chunk.reshape(4, HALF, HD)


def row_mask(half):
    position = lax.broadcasted_iota(jnp.int32, (MID, HD), 0)
    thi, s, tx, i = position >> 9, (position >> 6) & 7, (position >> 4) & 3, position & 15
    inside = half * HALF + i
    row = s * (8 * ROWS) + (thi * 4 + tx) * ROWS + inside
    return jnp.where((inside < ROWS) & (row < TILE), 1.0, 0.0).astype(F32)


def columns(rows):
    return jnp.concatenate([rows[:, g * HD : (g + 1) * HD].astype(F32).T for g in range(4)], axis=1)


def stacked(rows):
    return jnp.concatenate([rows[:, g * HD : (g + 1) * HD] for g in range(4)], axis=0)


def seen_row(ids_ref, count_ref, visible_ref, j):
    y, core, z = ids_ref[0], ids_ref[1], ids_ref[2]
    conv = jnp.where(z < 4, 2 * z, 15 - 2 * z)
    source = ((y - j) & 3) * 2 + core
    shift = jnp.int32(0)
    for i in range(1, 8):
        shift = jnp.where(source == i, SHIFT[i], shift)
    block = (z + shift) & 7
    seen = jnp.minimum(visible_ref[pl.ds(conv * 8 + block, 1), :], count_ref[conv])
    seen = jnp.where(seen > (y >> 1), 1.0, 0.0).astype(F32)
    return jnp.concatenate([seen] * 4, axis=1)


def masked_weights(keys_s, ok_s, q_t, rows):
    scores = dot(keys_s[rows, :], q_t)
    ok = ok_s[rows, :]
    return jnp.exp2(scores * SCALE_LOG2) * jnp.concatenate([ok] * 4, axis=1)


def load_pair(ids_ref, mine_ref, other_ref, keys_s, values_s, ok_s):
    core = ids_ref[1]

    @pl.when(core == 0)
    def _():
        keys_s[...] = mine_ref[...]
        values_s[...] = other_ref[...]

    @pl.when(core != 0)
    def _():
        keys_s[...] = other_ref[...]
        values_s[...] = mine_ref[...]

    ok_s[...] = row_mask(ids_ref[0] & 1)


def forward(ids_ref, count_ref, visible_ref, mine_ref, other_ref, q0, q1, q2, q3, acc_ref, sums_ref, keys_s, values_s, ok_s, turned_s, q_s):
    load_pair(ids_ref, mine_ref, other_ref, keys_s, values_s, ok_s)
    turned_s[...] = values_s[...].astype(F32).T.astype(BF16)
    for j, q in enumerate((q0, q1, q2, q3)):
        q_s[j] = q[...]

    def block(j, carry):
        q_t = columns(q_s[j, 0:128, :]).astype(BF16)
        o_t = columns(q_s[j, 128:256, :])
        total = jnp.zeros((1, 512), F32)
        acc = jnp.zeros((HD, 512), F32)
        for r in range(MID // CHUNK):
            rows = slice(r * CHUNK, (r + 1) * CHUNK)
            weights = masked_weights(keys_s, ok_s, q_t, rows)
            total = total + jnp.sum(weights, axis=0, keepdims=True)
            acc = acc + dot(turned_s[:, rows], weights.astype(BF16))
        seen = seen_row(ids_ref, count_ref, visible_ref, j)
        acc = acc * seen
        both = jnp.concatenate([total * seen, jnp.sum(acc * o_t, axis=0, keepdims=True)], axis=0)
        for to in range(Y):
            sums_ref[to, j] = both
        acc_ref[j] = acc
        return carry

    lax.fori_loop(0, Y, block, 0)


def all_sums(ids_ref, sums_ref, j):
    y = ids_ref[0]
    both = sums_ref[y, j]
    for k in range(1, Y):
        both = both + sums_ref[(y - k) & 3, (j - k) & 3]
    total = both[0:1]
    safe = jnp.where(total > 0, total, 1.0)
    return 1.0 / safe, both[1:2] / safe


def backward(
    ids_ref, count_ref, visible_ref, mine_ref, other_ref, q0, q1, q2, q3, acc_ref, sums_ref,
    r0, r1, r2, r3, keep_ref, send_ref, keys_s, values_s, ok_s, turned_s, q_s, dk_s, dv_s,
):
    load_pair(ids_ref, mine_ref, other_ref, keys_s, values_s, ok_s)
    turned_s[...] = keys_s[...].astype(F32).T.astype(BF16)
    dk_s[...] = jnp.zeros((MID, HD), F32)
    dv_s[...] = jnp.zeros((MID, HD), F32)
    for j, q in enumerate((q0, q1, q2, q3)):
        q_s[j] = q[...]

    def block(j, carry):
        q_t = columns(q_s[j, 0:128, :]).astype(BF16)
        o_t = columns(q_s[j, 128:256, :]).astype(BF16)
        q_rows = stacked(q_s[j, 0:128, :])
        o_rows = stacked(q_s[j, 128:256, :])
        inverse, delta = all_sums(ids_ref, sums_ref, j)
        acc = (acc_ref[j] * inverse).astype(BF16)
        inverse = inverse * seen_row(ids_ref, count_ref, visible_ref, j)
        dq = jnp.zeros((HD, 512), F32)
        for r in range(MID // CHUNK):
            rows = slice(r * CHUNK, (r + 1) * CHUNK)
            prob = masked_weights(keys_s, ok_s, q_t, rows) * inverse
            d_prob = dot(values_s[rows, :], o_t)
            d_score = (prob * (d_prob - delta)).astype(BF16)
            dk_s[rows, :] += dot(d_score, q_rows)
            dv_s[rows, :] += dot(prob.astype(BF16), o_rows)
            dq = dq + dot(turned_s[:, rows], d_score)
        q_s[j] = jnp.concatenate([acc, (dq * SCALE).astype(BF16)], axis=0)
        return carry

    lax.fori_loop(0, Y, block, 0)
    for j, r in enumerate((r0, r1, r2, r3)):
        r[...] = q_s[j]
    core = ids_ref[1]

    @pl.when(core == 0)
    def _():
        keep_ref[...] = dk_s[...] * SCALE
        send_ref[...] = dv_s[...].astype(BF16)

    @pl.when(core != 0)
    def _():
        keep_ref[...] = dv_s[...]
        send_ref[...] = (dk_s[...] * SCALE).astype(BF16)


def sum_tokens(gate_ref, r0, r1, r2, r3, out_ref):
    both = r0[...].astype(F32) + r1[...].astype(F32) + r2[...].astype(F32) + r3[...].astype(F32)
    for g in range(4):
        lanes = slice(g * HD, (g + 1) * HD)
        out_ref[0:128, lanes] = (both[0:128, lanes].T * gate_ref[0]).astype(BF16)
        out_ref[128:256, lanes] = both[128:256, lanes].T.astype(BF16)


def norm_back(x, d_normed, gain):
    mean_square = jnp.mean(x * x, axis=-1, keepdims=True)
    inverse = lax.rsqrt(mean_square + EPSILON)
    scaled = d_normed * gain
    dots = jnp.mean(x * scaled, axis=-1, keepdims=True)
    return inverse * scaled - x * (inverse * inverse * inverse * dots)


def finish_queries(queries_ref, got_ref, gain_ref, attended_ref, out_ref):
    gain = gain_ref[...]
    attended_ref[0] = got_ref[0:128, :]
    for g in range(4):
        lanes = slice(g * HD, (g + 1) * HD)
        x = queries_ref[0, :, lanes].astype(F32)
        out_ref[0, :, lanes] = norm_back(x, got_ref[128:256, lanes].astype(F32), gain).astype(BF16)


def finish_keys(keys_ref, got_ref, gain_ref, dk_ref, dv_ref):
    gain = gain_ref[...]
    for n in range(2):
        for head in range(8):
            hhi, hx = divmod(head, 4)
            lanes = slice(head * HD, (head + 1) * HD)
            for half, count in ((0, HALF), (1, ROWS - HALF)):
                at = (n * 2 + half) * 2
                rows = slice(half * HALF, half * HALF + count)
                piece = slice(hhi * HALF, hhi * HALF + count)
                dv_ref[n, rows, lanes] = got_ref[at + 1, hx, piece, :]
                x = keys_ref[n, rows, lanes].astype(F32)
                d_normed = got_ref[at, hx, piece, :].astype(F32)
                dk_ref[n, rows, lanes] = norm_back(x, d_normed, gain).astype(BF16)


def exchange(value, axes):
    return lax.all_to_all(value, axes, split_axis=0, concat_axis=0, tiled=True)


def rotated(value, k):
    return lax.ppermute(value, "y", [(i, (i + k) % Y) for i in range(Y)])


def swapped(value):
    return lax.ppermute(value, "core", [(0, 1), (1, 0)])


TO_PLANE = [(c * 8 + (z + SHIFT[i]) % 8, i * 8 + z) for i in range(8) for z, c in enumerate(CONV_OF)]
FROM_PLANE = [(b, a) for a, b in TO_PLANE]
PLANES = ("y", "core", "seq")


def shards(queries, keys, values, q_gain, k_gain, gate, tile_count, tile_owner, visible, d_out):
    y, core, z = lax.axis_index("y"), lax.axis_index("core"), lax.axis_index("seq")
    ids = jnp.stack([y, core, z]).astype(jnp.int32)
    gate_value = jnp.tanh(gate)
    q_gain = q_gain.reshape(1, HD)
    k_gain = k_gain.reshape(1, HD)
    owner = lax.dynamic_index_in_dim(tile_owner, y // 2, 1, keepdims=False)
    seen = visible.reshape(64, 128)

    (packed,) = call(pack_queries, [shape((256, 512), BF16)], gate_value, queries, d_out, q_gain, smem=1)
    packed, keys, values = lax.optimization_barrier((packed, keys, values))
    q0 = lax.ppermute(packed, PLANES, TO_PLANE)
    (packed_kv,) = call(pack_keys, [shape((8, 4, 32, HD), BF16)], keys, values, k_gain)
    got = exchange(packed_kv.reshape(32, 32, HD), ("y", "core", "x"))
    got, q0 = lax.optimization_barrier((got, q0))
    (chosen,) = call(choose_tiles, [shape((2, 8, 64, HD), BF16)], owner, got.reshape(8, 4, 32, HD), smem=1)
    mine = exchange(chosen.reshape(16, 64, HD), ("zhi", "seq")).reshape(MID, HD)
    q1, q2, q3 = rotated(q0, 1), rotated(q0, 2), rotated(q0, 3)
    other = swapped(mine)

    common = [pltpu.VMEM((MID, HD), BF16), pltpu.VMEM((MID, HD), BF16), pltpu.VMEM((MID, HD), F32)]
    common += [pltpu.VMEM((HD, MID), BF16), pltpu.VMEM((Y, 256, 512), BF16)]
    acc, sums = call(
        forward,
        [shape((Y, HD, 512), F32), shape((Y, Y, 2, 512), F32)],
        ids, tile_count, seen, mine, other, q0, q1, q2, q3,
        smem=2, scratch=common, flops=2 * 2 * 2048 * MID * HD, limit=32 << 20,
    )
    sums = exchange(sums, "y")
    r0, r1, r2, r3, keep, send = call(
        backward,
        [shape((256, 512), BF16)] * 4 + [shape((MID, HD), F32), shape((MID, HD), BF16)],
        ids, tile_count, seen, mine, other, q0, q1, q2, q3, acc, sums,
        smem=2, scratch=common + [pltpu.VMEM((MID, HD), F32)] * 2, flops=5 * 2 * 2048 * MID * HD, limit=32 << 20,
    )

    grads = (keep + swapped(send).astype(F32)).astype(BF16)
    back = exchange(grads.reshape(16, 64, HD), ("zhi", "seq"))
    r1, r2, r3 = rotated(r1, 3), rotated(r2, 2), rotated(r3, 1)
    (summed,) = call(sum_tokens, [shape((256, 512), BF16)], gate_value, r0, r1, r2, r3, smem=1)
    summed = lax.ppermute(summed, PLANES, FROM_PLANE)
    (placed,) = call(return_tiles, [shape((8, 4, 32, HD), BF16)], owner, back.reshape(2, 8, 64, HD), smem=1)
    home = exchange(placed.reshape(32, 32, HD), ("y", "core", "x")).reshape(8, 4, 32, HD)
    d_keys, d_values = call(finish_keys, [shape(keys.shape, BF16), shape(values.shape, BF16)], keys, home, k_gain)
    attended, d_queries = call(finish_queries, [shape(queries.shape, BF16)] * 2, queries, summed, q_gain)
    return (attended, d_queries, d_keys, d_values)


def solution(mesh):
    parts = Mesh(mesh.devices.reshape(Y, CORE, Z, 2, 4), ("y", "core", "seq", "zhi", "x"))
    conv, tensor = ("y", "core"), ("zhi", "x")
    tokens = P(conv, "seq", tensor)
    rows = P(conv, ("seq", "zhi", "x"), None)
    in_specs = (tokens, rows, rows, P(), P(), P(), P(), P(), P(), tokens)
    out_specs = (tokens, tokens, rows, rows)
    return jax.shard_map(shards, mesh=parts, in_specs=in_specs, out_specs=out_specs, check_vma=False)
```

```python
import math

import jax
import jax.numpy as jnp
from jax import lax
from jax.experimental import pallas as pl
from jax.experimental.pallas import tpu as pltpu
from jax.sharding import Mesh, PartitionSpec as P

HD = 128
TILE = 1601
ROWS = 26
HALF = 16
EPSILON = 1e-05
SCALE = 1.0 / math.sqrt(HD)
SCALE_LOG2 = SCALE / math.log(2.0)
F32 = jnp.float32
BF16 = jnp.bfloat16

Y, CORE, Z, N_O, N_C = 4, 2, 8, 8, 8
PLANE_OF = (0, 7, 1, 6, 2, 5, 3, 4)
CONV_OF = tuple(PLANE_OF.index(z) for z in range(Z))
SHIFT = (0, 4, 1, 3, 2, 6, 5, 7)
CHUNK = 256
MID = 1024


def dot(a, b):
    return jnp.dot(a, b, preferred_element_type=F32)


def call(kernel, outs, *args, smem=0, hbm=0, scratch=(), flops=0, limit=8 << 20):
    specs = [pl.BlockSpec(memory_space=pltpu.SMEM)] * smem
    specs += [pl.BlockSpec(memory_space=pltpu.HBM)] * hbm
    specs += [pl.BlockSpec(memory_space=pltpu.VMEM)] * (len(args) - smem - hbm)
    size = sum(a.size * a.dtype.itemsize for a in args) + sum(o.size * o.dtype.itemsize for o in outs)
    return pl.pallas_call(
        kernel,
        out_shape=outs,
        in_specs=specs,
        out_specs=[pl.BlockSpec(memory_space=pltpu.VMEM)] * len(outs),
        scratch_shapes=list(scratch),
        cost_estimate=pl.CostEstimate(flops=flops, bytes_accessed=size, transcendentals=0),
        compiler_params=pltpu.CompilerParams(vmem_limit_bytes=limit),
    )(*args)


def shape(dims, dtype):
    return jax.ShapeDtypeStruct(dims, dtype)


def gate_value(gate_ref):
    return jnp.tanh(jnp.full((1, HD), gate_ref[0], F32))


def pack_queries(gate_ref, queries_ref, d_out_ref, q_gain_ref, k_gain_ref, out_ref, gains_ref, x_s, d_s, sems):
    copies = [
        pltpu.make_async_copy(source, target, sems.at[i])
        for i, (source, target) in enumerate(
            ((queries_ref.at[0], x_s), (d_out_ref.at[0], d_s), (q_gain_ref, gains_ref.at[0:1]), (k_gain_ref, gains_ref.at[1:2]))
        )
    ]
    for copy in copies:
        copy.start()
    gate = gate_value(gate_ref)
    for copy in copies:
        copy.wait()
    gain = gains_ref[0:1]
    for g in range(4):
        lanes = slice(g * HD, (g + 1) * HD)
        x = x_s[:, lanes].astype(F32)
        mean_square = jnp.mean(x * x, axis=-1, keepdims=True)
        out_ref[0:128, lanes] = (x * lax.rsqrt(mean_square + EPSILON) * gain).astype(BF16)
        out_ref[128:256, lanes] = (gate * d_s[:, lanes].astype(F32)).astype(BF16)


def pack_keys(keys_ref, values_ref, gains_ref, out_ref):
    gain = gains_ref[1:2]
    for n in range(2):
        for head in range(8):
            hhi, hx = divmod(head, 4)
            lanes = slice(head * HD, (head + 1) * HD)
            x = keys_ref[n, :, lanes].astype(F32)
            mean_square = jnp.mean(x * x, axis=-1, keepdims=True)
            normed = (x * lax.rsqrt(mean_square + EPSILON) * gain).astype(BF16)
            pad = jnp.zeros((2 * HALF - ROWS, HD), BF16)
            for kv, rows in ((0, normed), (1, values_ref[n, :, lanes])):
                for half in range(2):
                    at = (n * 2 + half) * 2 + kv
                    if half == 0:
                        out_ref[at, hx, hhi * HALF : (hhi + 1) * HALF, :] = rows[:HALF]
                    else:
                        out_ref[at, hx, hhi * HALF : (hhi + 1) * HALF, :] = jnp.concatenate([rows[HALF:], pad], axis=0)


def choose_tiles(owner_ref, got_ref, out_ref):
    for z in range(Z):
        o = jnp.maximum(owner_ref[CONV_OF[z]], 0)
        chunk = got_ref[o]
        for hhi in range(2):
            out_ref[hhi, z] = chunk[:, hhi * HALF : (hhi + 1) * HALF, :].reshape(4 * HALF, HD)


def return_tiles(owner_ref, got_ref, out_ref):
    for o in range(N_O):
        found = jnp.int32(-1)
        for c in range(N_C):
            found = jnp.where(owner_ref[c] == o, PLANE_OF[c], found)
        at = jnp.maximum(found, 0)
        for hhi in range(2):
            chunk = jnp.where(found >= 0, got_ref[hhi, at].astype(F32), 0.0).astype(BF16)
            out_ref[o, :, hhi * HALF : (hhi + 1) * HALF, :] = chunk.reshape(4, HALF, HD)


def row_mask(half, dims, axis):
    position = lax.broadcasted_iota(jnp.int32, dims, axis)
    thi, s, tx, i = position >> 9, (position >> 6) & 7, (position >> 4) & 3, position & 15
    inside = half * HALF + i
    row = s * (8 * ROWS) + (thi * 4 + tx) * ROWS + inside
    return jnp.where((inside < ROWS) & (row < TILE), 1.0, 0.0).astype(F32)


def columns(rows):
    return jnp.concatenate([rows[:, g * HD : (g + 1) * HD].astype(F32).T for g in range(4)], axis=1)


def stacked(rows):
    return jnp.concatenate([rows[:, g * HD : (g + 1) * HD] for g in range(4)], axis=0)


def seen_row(ids_ref, count_ref, visible_ref, j):
    y, core, z = ids_ref[0], ids_ref[1], ids_ref[2]
    conv = jnp.where(z < 4, 2 * z, 15 - 2 * z)
    source = ((y - j) & 3) * 2 + core
    shift = jnp.int32(0)
    for i in range(1, 8):
        shift = jnp.where(source == i, SHIFT[i], shift)
    block = (z + shift) & 7
    seen = jnp.minimum(visible_ref[pl.ds(conv * 8 + block, 1), :], count_ref[conv])
    seen = jnp.where(seen > (y >> 1), 1.0, 0.0).astype(F32)
    return jnp.concatenate([seen] * 4, axis=1)


def weights_of(keys_s, q_t, rows):
    return jnp.exp2(dot(keys_s[rows, :], q_t) * SCALE_LOG2)


def load_pair(ids_ref, mine_ref, other_ref, keys_s, values_s):
    core = ids_ref[1]

    @pl.when(core == 0)
    def _():
        keys_s[...] = mine_ref[...]
        values_s[...] = other_ref[...]

    @pl.when(core != 0)
    def _():
        keys_s[...] = other_ref[...]
        values_s[...] = mine_ref[...]

    return row_mask(ids_ref[0] & 1, (MID, HD), 0)


def forward(ids_ref, count_ref, visible_ref, mine_ref, other_ref, q0, q1, q2, q3, acc_ref, sums_ref, keys_s, values_s, turned_s, q_s):
    ok = load_pair(ids_ref, mine_ref, other_ref, keys_s, values_s)
    keys_s[...] = (keys_s[...].astype(F32) * ok).astype(BF16)
    turned_s[0:HD, :] = (values_s[...].astype(F32) * ok).T.astype(BF16)
    turned_s[HD:, :] = row_mask(ids_ref[0] & 1, (16, MID), 1).astype(BF16)
    for j, q in enumerate((q0, q1, q2, q3)):
        q_s[j] = q[...]

    def block(j, carry):
        q_t = columns(q_s[j, 0:128, :]).astype(BF16)
        o_t = columns(q_s[j, 128:256, :])
        acc = jnp.zeros((HD + 16, 512), F32)
        for r in range(MID // CHUNK):
            rows = slice(r * CHUNK, (r + 1) * CHUNK)
            acc = acc + dot(turned_s[:, rows], weights_of(keys_s, q_t, rows).astype(BF16))
        acc = acc * seen_row(ids_ref, count_ref, visible_ref, j)
        both = jnp.concatenate([acc[HD : HD + 1], jnp.sum(acc[:HD] * o_t, axis=0, keepdims=True)], axis=0)
        for to in range(Y):
            sums_ref[to, j] = both
        acc_ref[j] = acc[:HD]
        return carry

    lax.fori_loop(0, Y, block, 0)


def all_sums(ids_ref, sums_ref, j):
    y = ids_ref[0]
    both = sums_ref[y, j]
    for k in range(1, Y):
        both = both + sums_ref[(y - k) & 3, (j - k) & 3]
    total = both[0:1]
    safe = jnp.where(total > 0, total, 1.0)
    return 1.0 / safe, both[1:2] / safe


def backward(
    ids_ref, count_ref, visible_ref, mine_ref, other_ref, q0, q1, q2, q3, acc_ref, sums_ref,
    r0, r1, r2, r3, keep_ref, send_ref, keys_s, values_s, turned_s, q_s, dk_s, dv_s,
):
    ok = load_pair(ids_ref, mine_ref, other_ref, keys_s, values_s)
    masked = keys_s[...].astype(F32) * ok
    keys_s[...] = masked.astype(BF16)
    turned_s[...] = masked.T.astype(BF16)
    dk_s[...] = jnp.zeros((MID, HD), F32)
    dv_s[...] = jnp.zeros((MID, HD), F32)
    for j, q in enumerate((q0, q1, q2, q3)):
        q_s[j] = q[...]

    def block(j, carry):
        q_t = columns(q_s[j, 0:128, :]).astype(BF16)
        o_t = columns(q_s[j, 128:256, :]).astype(BF16)
        q_rows = stacked(q_s[j, 0:128, :])
        o_rows = stacked(q_s[j, 128:256, :])
        inverse, delta = all_sums(ids_ref, sums_ref, j)
        acc = (acc_ref[j] * inverse).astype(BF16)
        inverse = inverse * seen_row(ids_ref, count_ref, visible_ref, j)
        dq = jnp.zeros((HD, 512), F32)
        for r in range(MID // CHUNK):
            rows = slice(r * CHUNK, (r + 1) * CHUNK)
            prob = weights_of(keys_s, q_t, rows) * inverse
            d_prob = dot(values_s[rows, :], o_t)
            d_score = (prob * (d_prob - delta)).astype(BF16)
            dk_s[rows, :] += dot(d_score, q_rows)
            dv_s[rows, :] += dot(prob.astype(BF16), o_rows)
            dq = dq + dot(turned_s[:, rows], d_score)
        q_s[j] = jnp.concatenate([acc, (dq * SCALE).astype(BF16)], axis=0)
        return carry

    lax.fori_loop(0, Y, block, 0)
    for j, r in enumerate((r0, r1, r2, r3)):
        r[...] = q_s[j]
    core = ids_ref[1]

    @pl.when(core == 0)
    def _():
        keep_ref[...] = dk_s[...] * (ok * SCALE)
        send_ref[...] = (dv_s[...] * ok).astype(BF16)

    @pl.when(core != 0)
    def _():
        keep_ref[...] = dv_s[...] * ok
        send_ref[...] = (dk_s[...] * (ok * SCALE)).astype(BF16)


def sum_tokens(gate_ref, r0, r1, r2, r3, out_ref):
    gate = gate_value(gate_ref)
    both = r0[...].astype(F32) + r1[...].astype(F32) + r2[...].astype(F32) + r3[...].astype(F32)
    for g in range(4):
        lanes = slice(g * HD, (g + 1) * HD)
        out_ref[0:128, lanes] = (both[0:128, lanes].T * gate).astype(BF16)
        out_ref[128:256, lanes] = both[128:256, lanes].T.astype(BF16)


def norm_back(x, d_normed, gain):
    mean_square = jnp.mean(x * x, axis=-1, keepdims=True)
    inverse = lax.rsqrt(mean_square + EPSILON)
    scaled = d_normed * gain
    dots = jnp.mean(x * scaled, axis=-1, keepdims=True)
    return inverse * scaled - x * (inverse * inverse * inverse * dots)


def finish_queries(queries_ref, got_ref, gains_ref, attended_ref, out_ref):
    gain = gains_ref[0:1]
    attended_ref[0] = got_ref[0:128, :]
    for g in range(4):
        lanes = slice(g * HD, (g + 1) * HD)
        x = queries_ref[0, :, lanes].astype(F32)
        out_ref[0, :, lanes] = norm_back(x, got_ref[128:256, lanes].astype(F32), gain).astype(BF16)


def finish_keys(keys_ref, got_ref, gains_ref, dk_ref, dv_ref):
    gain = gains_ref[1:2]
    for n in range(2):
        for head in range(8):
            hhi, hx = divmod(head, 4)
            lanes = slice(head * HD, (head + 1) * HD)
            for half, count in ((0, HALF), (1, ROWS - HALF)):
                at = (n * 2 + half) * 2
                rows = slice(half * HALF, half * HALF + count)
                piece = slice(hhi * HALF, hhi * HALF + count)
                dv_ref[n, rows, lanes] = got_ref[at + 1, hx, piece, :]
                x = keys_ref[n, rows, lanes].astype(F32)
                d_normed = got_ref[at, hx, piece, :].astype(F32)
                dk_ref[n, rows, lanes] = norm_back(x, d_normed, gain).astype(BF16)


def exchange(value, axes):
    return lax.all_to_all(value, axes, split_axis=0, concat_axis=0, tiled=True)


def rotated(value, k):
    return lax.ppermute(value, "y", [(i, (i + k) % Y) for i in range(Y)])


def swapped(value):
    return lax.ppermute(value, "core", [(0, 1), (1, 0)])


TO_PLANE = [(c * 8 + (z + SHIFT[i]) % 8, i * 8 + z) for i in range(8) for z, c in enumerate(CONV_OF)]
FROM_PLANE = [(b, a) for a, b in TO_PLANE]
PLANES = ("y", "core", "seq")


def shards(queries, keys, values, q_gain, k_gain, gate, tile_count, tile_owner, visible, d_out):
    y, core, z = lax.axis_index("y"), lax.axis_index("core"), lax.axis_index("seq")
    ids = jnp.stack([y, core, z]).astype(jnp.int32)
    q_gain = q_gain.reshape(1, HD)
    k_gain = k_gain.reshape(1, HD)
    owner = lax.dynamic_index_in_dim(tile_owner, y // 2, 1, keepdims=False)
    seen = visible.reshape(64, 128)

    buffers = [pltpu.VMEM((128, 512), BF16), pltpu.VMEM((128, 512), BF16), pltpu.SemaphoreType.DMA((4,))]
    packed, gains = call(
        pack_queries,
        [shape((256, 512), BF16), shape((2, HD), F32)],
        gate, queries, d_out, q_gain, k_gain,
        smem=1, hbm=4, scratch=buffers, limit=60 << 20,
    )
    q0 = lax.ppermute(packed, PLANES, TO_PLANE)
    (packed_kv,) = call(pack_keys, [shape((8, 4, 32, HD), BF16)], keys, values, gains)
    got = exchange(packed_kv.reshape(32, 32, HD), ("y", "core", "x"))
    got, q0 = lax.optimization_barrier((got, q0))
    (chosen,) = call(choose_tiles, [shape((2, 8, 64, HD), BF16)], owner, got.reshape(8, 4, 32, HD), smem=1)
    mine = exchange(chosen.reshape(16, 64, HD), ("zhi", "seq")).reshape(MID, HD)
    q1, q2, q3 = rotated(q0, 1), rotated(q0, 2), rotated(q0, 3)
    other = swapped(mine)

    pair = [pltpu.VMEM((MID, HD), BF16), pltpu.VMEM((MID, HD), BF16)]
    tokens = pltpu.VMEM((Y, 256, 512), BF16)
    gradients = [pltpu.VMEM((MID, HD), F32), pltpu.VMEM((MID, HD), F32)]
    acc, sums = call(
        forward,
        [shape((Y, HD, 512), F32), shape((Y, Y, 2, 512), F32)],
        ids, tile_count, seen, mine, other, q0, q1, q2, q3,
        smem=2, scratch=pair + [pltpu.VMEM((HD + 16, MID), BF16), tokens], flops=2 * 2 * 2048 * MID * HD, limit=32 << 20,
    )
    sums = exchange(sums, "y")
    r0, r1, r2, r3, keep, send = call(
        backward,
        [shape((256, 512), BF16)] * 4 + [shape((MID, HD), F32), shape((MID, HD), BF16)],
        ids, tile_count, seen, mine, other, q0, q1, q2, q3, acc, sums,
        smem=2, scratch=pair + [pltpu.VMEM((HD, MID), BF16), tokens] + gradients, flops=5 * 2 * 2048 * MID * HD, limit=32 << 20,
    )

    grads = (keep + swapped(send).astype(F32)).astype(BF16)
    back = exchange(grads.reshape(16, 64, HD), ("zhi", "seq"))
    r1, r2, r3 = rotated(r1, 3), rotated(r2, 2), rotated(r3, 1)
    (placed,) = call(return_tiles, [shape((8, 4, 32, HD), BF16)], owner, back.reshape(2, 8, 64, HD), smem=1)
    home = exchange(placed.reshape(32, 32, HD), ("y", "core", "x")).reshape(8, 4, 32, HD)
    r1, r2, r3, placed = lax.optimization_barrier((r1, r2, r3, placed))
    (summed,) = call(sum_tokens, [shape((256, 512), BF16)], gate, r0, r1, r2, r3, smem=1)
    summed = lax.ppermute(summed, PLANES, FROM_PLANE)
    d_keys, d_values = call(finish_keys, [shape(keys.shape, BF16), shape(values.shape, BF16)], keys, home, gains)
    attended, d_queries = call(finish_queries, [shape(queries.shape, BF16)] * 2, queries, summed, gains)
    return (attended, d_queries, d_keys, d_values)


def solution(mesh):
    parts = Mesh(mesh.devices.reshape(Y, CORE, Z, 2, 4), ("y", "core", "seq", "zhi", "x"))
    conv, tensor = ("y", "core"), ("zhi", "x")
    tokens = P(conv, "seq", tensor)
    rows = P(conv, ("seq", "zhi", "x"), None)
    in_specs = (tokens, rows, rows, P(), P(), P(), P(), P(), P(), tokens)
    out_specs = (tokens, tokens, rows, rows)
    return jax.shard_map(shards, mesh=parts, in_specs=in_specs, out_specs=out_specs, check_vma=False)
```

```python
import math

import jax
import jax.numpy as jnp
from jax import lax
from jax.experimental import pallas as pl
from jax.experimental.pallas import tpu as pltpu
from jax.sharding import Mesh, PartitionSpec as P

HD = 128
TILE = 1601
ROWS = 26
HALF = 13
SLOT = 16
STEP = 14
EPSILON = 1e-05
SCALE = 1.0 / math.sqrt(HD)
SCALE_LOG2 = SCALE / math.log(2.0)
F32 = jnp.float32
BF16 = jnp.bfloat16

Y, CORE, Z, N_O, N_C = 4, 2, 8, 8, 8
PLANE_OF = (0, 7, 1, 6, 2, 5, 3, 4)
CONV_OF = tuple(PLANE_OF.index(z) for z in range(Z))
SHIFT = (0, 4, 1, 3, 2, 6, 5, 7)
BLOCK = 4 * STEP
MID = 2 * Z * BLOCK


def dot(a, b):
    return jnp.dot(a, b, preferred_element_type=F32)


def call(kernel, outs, *args, smem=0, hbm=0, scratch=(), flops=0, limit=8 << 20):
    specs = [pl.BlockSpec(memory_space=pltpu.SMEM)] * smem
    specs += [pl.BlockSpec(memory_space=pltpu.HBM)] * hbm
    specs += [pl.BlockSpec(memory_space=pltpu.VMEM)] * (len(args) - smem - hbm)
    size = sum(a.size * a.dtype.itemsize for a in args) + sum(o.size * o.dtype.itemsize for o in outs)
    return pl.pallas_call(
        kernel,
        out_shape=outs,
        in_specs=specs,
        out_specs=[pl.BlockSpec(memory_space=pltpu.VMEM)] * len(outs),
        scratch_shapes=list(scratch),
        cost_estimate=pl.CostEstimate(flops=flops, bytes_accessed=size, transcendentals=0),
        compiler_params=pltpu.CompilerParams(vmem_limit_bytes=limit),
    )(*args)


def shape(dims, dtype):
    return jax.ShapeDtypeStruct(dims, dtype)


def gate_value(gate_ref):
    return jnp.tanh(jnp.full((1, HD), gate_ref[0], F32))


def pack_queries(gate_ref, queries_ref, d_out_ref, q_gain_ref, k_gain_ref, out_ref, gains_ref, x_s, d_s, sems):
    copies = [
        pltpu.make_async_copy(source, target, sems.at[i])
        for i, (source, target) in enumerate(
            ((queries_ref.at[0], x_s), (d_out_ref.at[0], d_s), (q_gain_ref, gains_ref.at[0:1]), (k_gain_ref, gains_ref.at[1:2]))
        )
    ]
    for copy in copies:
        copy.start()
    gate = gate_value(gate_ref)
    for copy in copies:
        copy.wait()
    gain = gains_ref[0:1]
    for g in range(4):
        lanes = slice(g * HD, (g + 1) * HD)
        x = x_s[:, lanes].astype(F32)
        mean_square = jnp.mean(x * x, axis=-1, keepdims=True)
        out_ref[0:128, lanes] = (x * lax.rsqrt(mean_square + EPSILON) * gain).astype(BF16)
        out_ref[128:256, lanes] = (gate * d_s[:, lanes].astype(F32)).astype(BF16)


def pack_keys(keys_ref, values_ref, gains_ref, out_ref):
    gain = gains_ref[1:2]
    for n in range(2):
        for head in range(8):
            hhi, hx = divmod(head, 4)
            lanes = slice(head * HD, (head + 1) * HD)
            x = keys_ref[n, :, lanes].astype(F32)
            mean_square = jnp.mean(x * x, axis=-1, keepdims=True)
            normed = x * lax.rsqrt(mean_square + EPSILON) * gain
            pad = jnp.zeros((SLOT - HALF, HD), F32)
            for kv, rows in ((0, normed), (1, values_ref[n, :, lanes].astype(F32))):
                for half in range(2):
                    at = (n * 2 + half) * 2 + kv
                    piece = jnp.concatenate([rows[half * HALF : (half + 1) * HALF], pad], axis=0)
                    out_ref[at, hx, hhi * SLOT : (hhi + 1) * SLOT, :] = piece.astype(BF16)


def choose_tiles(owner_ref, got_ref, out_ref):
    for z in range(Z):
        o = jnp.maximum(owner_ref[CONV_OF[z]], 0)
        chunk = got_ref[o].astype(F32)
        for hhi in range(2):
            pieces = [chunk[tx, hhi * SLOT : hhi * SLOT + STEP, :] for tx in range(4)]
            out_ref[hhi, z] = jnp.concatenate(pieces, axis=0).astype(BF16)


def return_tiles(owner_ref, got_ref, out_ref):
    for o in range(N_O):
        found = jnp.int32(-1)
        for c in range(N_C):
            found = jnp.where(owner_ref[c] == o, PLANE_OF[c], found)
        at = jnp.maximum(found, 0)
        for hhi in range(2):
            chunk = jnp.where(found >= 0, got_ref[hhi, at].astype(F32), 0.0)
            pad = jnp.zeros((SLOT - STEP, HD), F32)
            for tx in range(4):
                piece = jnp.concatenate([chunk[tx * STEP : (tx + 1) * STEP], pad], axis=0)
                out_ref[o, tx, hhi * SLOT : (hhi + 1) * SLOT, :] = piece.astype(BF16)


def row_mask(half, dims, axis):
    def split(value, size):
        whole = jnp.floor((value + 0.5) * (1.0 / size))
        return whole, value - whole * size

    position = lax.broadcasted_iota(jnp.int32, dims, axis).astype(F32)
    group, inside = split(position, BLOCK)
    thi, s = split(group, Z)
    tx, i = split(inside, STEP)
    row = s * (8 * ROWS) + (thi * 4 + tx) * ROWS + (i + (half * HALF).astype(F32))
    return jnp.where((i < HALF - 0.5) & (row < TILE - 0.5), 1.0, 0.0).astype(F32)


def columns(rows):
    return jnp.concatenate([rows[:, g * HD : (g + 1) * HD].astype(F32).T for g in range(4)], axis=1)


def stacked(rows):
    return jnp.concatenate([rows[:, g * HD : (g + 1) * HD] for g in range(4)], axis=0)


def seen_row(ids_ref, count_ref, visible_ref, j):
    y, core, z = ids_ref[0], ids_ref[1], ids_ref[2]
    conv = jnp.where(z < 4, 2 * z, 15 - 2 * z)
    source = ((y - j) & 3) * 2 + core
    shift = jnp.int32(0)
    for i in range(1, 8):
        shift = jnp.where(source == i, SHIFT[i], shift)
    block = (z + shift) & 7
    seen = jnp.minimum(visible_ref[pl.ds(conv * 8 + block, 1), :], count_ref[conv])
    seen = jnp.where(seen > (y >> 1), 1.0, 0.0).astype(F32)
    return jnp.concatenate([seen] * 4, axis=1)


def weights_of(keys_s, q_t):
    return jnp.exp2(dot(keys_s[...], q_t) * SCALE_LOG2)


def load_pair(ids_ref, mine_ref, other_ref, keys_s, values_s):
    core = ids_ref[1]

    @pl.when(core == 0)
    def _():
        keys_s[...] = mine_ref[...]
        values_s[...] = other_ref[...]

    @pl.when(core != 0)
    def _():
        keys_s[...] = other_ref[...]
        values_s[...] = mine_ref[...]

    return row_mask(ids_ref[0] & 1, (MID, HD), 0)


def forward(ids_ref, count_ref, visible_ref, mine_ref, other_ref, q0, q1, q2, q3, acc_ref, sums_ref, keys_s, values_s, turned_s, q_s):
    ok = load_pair(ids_ref, mine_ref, other_ref, keys_s, values_s)
    keys_s[...] = (keys_s[...].astype(F32) * ok).astype(BF16)
    turned_s[0:HD, :] = (values_s[...].astype(F32) * ok).T.astype(BF16)
    turned_s[HD:, :] = row_mask(ids_ref[0] & 1, (16, MID), 1).astype(BF16)
    for j, q in enumerate((q0, q1, q2, q3)):
        q_s[j] = q[...]

    def block(j, carry):
        q_t = columns(q_s[j, 0:128, :]).astype(BF16)
        o_t = columns(q_s[j, 128:256, :])
        acc = dot(turned_s[...], weights_of(keys_s, q_t).astype(BF16))
        acc = acc * seen_row(ids_ref, count_ref, visible_ref, j)
        both = jnp.concatenate([acc[HD : HD + 1], jnp.sum(acc[:HD] * o_t, axis=0, keepdims=True)], axis=0)
        for to in range(Y):
            sums_ref[to, j] = both
        acc_ref[j] = acc[:HD]
        return carry

    lax.fori_loop(0, Y, block, 0, unroll=True)


def all_sums(ids_ref, sums_ref, j):
    y = ids_ref[0]
    both = sums_ref[y, j]
    for k in range(1, Y):
        both = both + sums_ref[(y - k) & 3, (j - k) & 3]
    total = both[0:1]
    safe = jnp.where(total > 0, total, 1.0)
    return 1.0 / safe, both[1:2] / safe


def backward(
    ids_ref, count_ref, visible_ref, mine_ref, other_ref, q0, q1, q2, q3, acc_ref, sums_ref,
    r0, r1, r2, r3, keep_ref, send_ref, keys_s, values_s, turned_s, q_s, dk_s, dv_s,
):
    ok = load_pair(ids_ref, mine_ref, other_ref, keys_s, values_s)
    masked = keys_s[...].astype(F32) * ok
    keys_s[...] = masked.astype(BF16)
    turned_s[...] = masked.T.astype(BF16)
    dk_s[...] = jnp.zeros((MID, HD), F32)
    dv_s[...] = jnp.zeros((MID, HD), F32)
    for j, q in enumerate((q0, q1, q2, q3)):
        q_s[j] = q[...]

    def block(j, carry):
        q_t = columns(q_s[j, 0:128, :]).astype(BF16)
        o_t = columns(q_s[j, 128:256, :]).astype(BF16)
        q_rows = stacked(q_s[j, 0:128, :])
        o_rows = stacked(q_s[j, 128:256, :])
        inverse, delta = all_sums(ids_ref, sums_ref, j)
        acc = (acc_ref[j] * inverse).astype(BF16)
        inverse = inverse * seen_row(ids_ref, count_ref, visible_ref, j)
        prob = weights_of(keys_s, q_t) * inverse
        d_score = (prob * (dot(values_s[...], o_t) - delta)).astype(BF16)
        dk_s[...] += dot(d_score, q_rows)
        dv_s[...] += dot(prob.astype(BF16), o_rows)
        dq = dot(turned_s[...], d_score)
        q_s[j] = jnp.concatenate([acc, (dq * SCALE).astype(BF16)], axis=0)
        return carry

    lax.fori_loop(0, Y, block, 0, unroll=2)
    for j, r in enumerate((r0, r1, r2, r3)):
        r[...] = q_s[j]
    core = ids_ref[1]

    @pl.when(core == 0)
    def _():
        keep_ref[...] = dk_s[...] * (ok * SCALE)
        send_ref[...] = (dv_s[...] * ok).astype(BF16)

    @pl.when(core != 0)
    def _():
        keep_ref[...] = dv_s[...] * ok
        send_ref[...] = (dk_s[...] * (ok * SCALE)).astype(BF16)


def sum_tokens(gate_ref, r0, r1, r2, r3, out_ref):
    gate = gate_value(gate_ref)
    both = r0[...].astype(F32) + r1[...].astype(F32) + r2[...].astype(F32) + r3[...].astype(F32)
    for g in range(4):
        lanes = slice(g * HD, (g + 1) * HD)
        out_ref[0:128, lanes] = (both[0:128, lanes].T * gate).astype(BF16)
        out_ref[128:256, lanes] = both[128:256, lanes].T.astype(BF16)


def norm_back(x, d_normed, gain):
    mean_square = jnp.mean(x * x, axis=-1, keepdims=True)
    inverse = lax.rsqrt(mean_square + EPSILON)
    scaled = d_normed * gain
    dots = jnp.mean(x * scaled, axis=-1, keepdims=True)
    return inverse * scaled - x * (inverse * inverse * inverse * dots)


def finish_queries(queries_ref, got_ref, gains_ref, attended_ref, out_ref):
    gain = gains_ref[0:1]
    attended_ref[0] = got_ref[0:128, :]
    for g in range(4):
        lanes = slice(g * HD, (g + 1) * HD)
        x = queries_ref[0, :, lanes].astype(F32)
        out_ref[0, :, lanes] = norm_back(x, got_ref[128:256, lanes].astype(F32), gain).astype(BF16)


def finish_keys(keys_ref, got_ref, gains_ref, dk_ref, dv_ref):
    gain = gains_ref[1:2]
    for n in range(2):
        for head in range(8):
            hhi, hx = divmod(head, 4)
            lanes = slice(head * HD, (head + 1) * HD)
            x = keys_ref[n, :, lanes].astype(F32)

            def rows(kv):
                halves = [got_ref[(n * 2 + half) * 2 + kv, hx, hhi * SLOT : (hhi + 1) * SLOT, :].astype(F32) for half in range(2)]
                return jnp.concatenate([piece[:HALF] for piece in halves], axis=0)

            dk_ref[n, :, lanes] = norm_back(x, rows(0), gain).astype(BF16)
            dv_ref[n, :, lanes] = rows(1).astype(BF16)


def exchange(value, axes):
    return lax.all_to_all(value, axes, split_axis=0, concat_axis=0, tiled=True)


def rotated(value, k):
    return lax.ppermute(value, "y", [(i, (i + k) % Y) for i in range(Y)])


def swapped(value):
    return lax.ppermute(value, "core", [(0, 1), (1, 0)])


TO_PLANE = [(c * 8 + (z + SHIFT[i]) % 8, i * 8 + z) for i in range(8) for z, c in enumerate(CONV_OF)]
FROM_PLANE = [(b, a) for a, b in TO_PLANE]
PLANES = ("y", "core", "seq")


def shards(queries, keys, values, q_gain, k_gain, gate, tile_count, tile_owner, visible, d_out):
    y, core, z = lax.axis_index("y"), lax.axis_index("core"), lax.axis_index("seq")
    ids = jnp.stack([y, core, z]).astype(jnp.int32)
    q_gain = q_gain.reshape(1, HD)
    k_gain = k_gain.reshape(1, HD)
    owner = lax.dynamic_index_in_dim(tile_owner, y // 2, 1, keepdims=False)
    seen = visible.reshape(64, 128)

    buffers = [pltpu.VMEM((128, 512), BF16), pltpu.VMEM((128, 512), BF16), pltpu.SemaphoreType.DMA((4,))]
    packed, gains = call(
        pack_queries,
        [shape((256, 512), BF16), shape((2, HD), F32)],
        gate, queries, d_out, q_gain, k_gain,
        smem=1, hbm=4, scratch=buffers, limit=60 << 20,
    )
    q0 = lax.ppermute(packed, PLANES, TO_PLANE)
    (packed_kv,) = call(pack_keys, [shape((8, 4, 32, HD), BF16)], keys, values, gains)
    got = exchange(packed_kv.reshape(32, 32, HD), ("y", "core", "x"))
    got, q0 = lax.optimization_barrier((got, q0))
    (chosen,) = call(choose_tiles, [shape((2, 8, BLOCK, HD), BF16)], owner, got.reshape(8, 4, 32, HD), smem=1)
    mine = exchange(chosen.reshape(16, BLOCK, HD), ("zhi", "seq")).reshape(MID, HD)
    q1, q2, q3 = rotated(q0, 1), rotated(q0, 2), rotated(q0, 3)
    other = swapped(mine)

    pair = [pltpu.VMEM((MID, HD), BF16), pltpu.VMEM((MID, HD), BF16)]
    tokens = pltpu.VMEM((Y, 256, 512), BF16)
    gradients = [pltpu.VMEM((MID, HD), F32), pltpu.VMEM((MID, HD), F32)]
    acc, sums = call(
        forward,
        [shape((Y, HD, 512), F32), shape((Y, Y, 2, 512), F32)],
        ids, tile_count, seen, mine, other, q0, q1, q2, q3,
        smem=2, scratch=pair + [pltpu.VMEM((HD + 16, MID), BF16), tokens], flops=2 * 2 * 2048 * MID * HD, limit=32 << 20,
    )
    sums = exchange(sums, "y")
    r0, r1, r2, r3, keep, send = call(
        backward,
        [shape((256, 512), BF16)] * 4 + [shape((MID, HD), F32), shape((MID, HD), BF16)],
        ids, tile_count, seen, mine, other, q0, q1, q2, q3, acc, sums,
        smem=2, scratch=pair + [pltpu.VMEM((HD, MID), BF16), tokens] + gradients, flops=5 * 2 * 2048 * MID * HD, limit=32 << 20,
    )

    grads = (keep + swapped(send).astype(F32)).astype(BF16)
    back = exchange(grads.reshape(16, BLOCK, HD), ("zhi", "seq"))
    r1, r2, r3 = rotated(r1, 3), rotated(r2, 2), rotated(r3, 1)
    (placed,) = call(return_tiles, [shape((8, 4, 32, HD), BF16)], owner, back.reshape(2, 8, BLOCK, HD), smem=1)
    home = exchange(placed.reshape(32, 32, HD), ("y", "core", "x")).reshape(8, 4, 32, HD)
    r1, r2, r3, placed = lax.optimization_barrier((r1, r2, r3, placed))
    (summed,) = call(sum_tokens, [shape((256, 512), BF16)], gate, r0, r1, r2, r3, smem=1)
    summed = lax.ppermute(summed, PLANES, FROM_PLANE)
    d_keys, d_values = call(finish_keys, [shape(keys.shape, BF16), shape(values.shape, BF16)], keys, home, gains, flops=20_000_000_000)
    attended, d_queries = call(finish_queries, [shape(queries.shape, BF16)] * 2, queries, summed, gains)
    return (attended, d_queries, d_keys, d_values)


def solution(mesh):
    parts = Mesh(mesh.devices.reshape(Y, CORE, Z, 2, 4), ("y", "core", "seq", "zhi", "x"))
    conv, tensor = ("y", "core"), ("zhi", "x")
    tokens = P(conv, "seq", tensor)
    rows = P(conv, ("seq", "zhi", "x"), None)
    in_specs = (tokens, rows, rows, P(), P(), P(), P(), P(), P(), tokens)
    out_specs = (tokens, tokens, rows, rows)
    return jax.shard_map(shards, mesh=parts, in_specs=in_specs, out_specs=out_specs, check_vma=False)
```

```python
import math

import jax
import jax.numpy as jnp
from jax import lax
from jax.experimental import pallas as pl
from jax.experimental.pallas import tpu as pltpu
from jax.sharding import Mesh, PartitionSpec as P

HD = 128
TILE = 1601
ROWS = 26
HALF = 13
SLOT = 16
STEP = 14
EPSILON = 1e-05
SCALE = 1.0 / math.sqrt(HD)
SCALE_LOG2 = SCALE / math.log(2.0)
F32 = jnp.float32
BF16 = jnp.bfloat16

Y, CORE, Z, N_O, N_C = 4, 2, 8, 8, 8
PLANE_OF = (0, 7, 1, 6, 3, 4, 2, 5)
CONV_OF = tuple(PLANE_OF.index(z) for z in range(Z))
SHIFT = (0, 4, 1, 3, 5, 7, 2, 6)
MIXED = 160
BLOCK = 4 * STEP
MID = 2 * Z * BLOCK


def dot(a, b):
    return jnp.dot(a, b, preferred_element_type=F32)


def call(kernel, outs, *args, smem=0, hbm=0, scratch=(), flops=0, limit=8 << 20):
    specs = [pl.BlockSpec(memory_space=pltpu.SMEM)] * smem
    specs += [pl.BlockSpec(memory_space=pltpu.HBM)] * hbm
    specs += [pl.BlockSpec(memory_space=pltpu.VMEM)] * (len(args) - smem - hbm)
    size = sum(a.size * a.dtype.itemsize for a in args) + sum(o.size * o.dtype.itemsize for o in outs)
    return pl.pallas_call(
        kernel,
        out_shape=outs,
        in_specs=specs,
        out_specs=[pl.BlockSpec(memory_space=pltpu.VMEM)] * len(outs),
        scratch_shapes=list(scratch),
        cost_estimate=pl.CostEstimate(flops=flops, bytes_accessed=size, transcendentals=0),
        compiler_params=pltpu.CompilerParams(vmem_limit_bytes=limit),
    )(*args)


def shape(dims, dtype):
    return jax.ShapeDtypeStruct(dims, dtype)


def gate_value(gate_ref):
    return jnp.tanh(jnp.full((1, HD), gate_ref[0], F32))


def pack_queries(gate_ref, queries_ref, d_out_ref, q_gain_ref, k_gain_ref, out_ref, gains_ref, x_s, d_s, sems):
    copies = [
        pltpu.make_async_copy(source, target, sems.at[i])
        for i, (source, target) in enumerate(
            ((queries_ref.at[0], x_s), (d_out_ref.at[0], d_s), (q_gain_ref, gains_ref.at[0:1]), (k_gain_ref, gains_ref.at[1:2]))
        )
    ]
    for copy in copies:
        copy.start()
    gate = gate_value(gate_ref)
    for copy in copies:
        copy.wait()
    gain = gains_ref[0:1]
    for g in range(4):
        lanes = slice(g * HD, (g + 1) * HD)
        x = x_s[:, lanes].astype(F32)
        mean_square = jnp.mean(x * x, axis=-1, keepdims=True)
        out_ref[0:128, lanes] = (x * lax.rsqrt(mean_square + EPSILON) * gain).astype(BF16)
        out_ref[128:256, lanes] = (gate * d_s[:, lanes].astype(F32)).astype(BF16)


def pack_keys(keys_ref, values_ref, gains_ref, out_ref):
    gain = gains_ref[1:2]
    for n in range(2):
        for head in range(8):
            hhi, hx = divmod(head, 4)
            lanes = slice(head * HD, (head + 1) * HD)
            x = keys_ref[n, :, lanes].astype(F32)
            mean_square = jnp.mean(x * x, axis=-1, keepdims=True)
            normed = x * lax.rsqrt(mean_square + EPSILON) * gain
            pad = jnp.zeros((SLOT - HALF, HD), F32)
            for kv, rows in ((0, normed), (1, values_ref[n, :, lanes].astype(F32))):
                for half in range(2):
                    at = (n * 2 + half) * 2 + kv
                    piece = jnp.concatenate([rows[half * HALF : (half + 1) * HALF], pad], axis=0)
                    out_ref[at, hx, hhi * SLOT : (hhi + 1) * SLOT, :] = piece.astype(BF16)


def choose_tiles(owner_ref, got_ref, out_ref):
    for z in range(Z):
        o = jnp.maximum(owner_ref[CONV_OF[z]], 0)
        chunk = got_ref[o].astype(F32)
        for hhi in range(2):
            pieces = [chunk[tx, hhi * SLOT : hhi * SLOT + STEP, :] for tx in range(4)]
            out_ref[hhi, z] = jnp.concatenate(pieces, axis=0).astype(BF16)


def return_tiles(owner_ref, got_ref, out_ref):
    for o in range(N_O):
        found = jnp.int32(-1)
        for c in range(N_C):
            found = jnp.where(owner_ref[c] == o, PLANE_OF[c], found)
        at = jnp.maximum(found, 0)
        for hhi in range(2):
            chunk = jnp.where(found >= 0, got_ref[hhi, at].astype(F32), 0.0)
            pad = jnp.zeros((SLOT - STEP, HD), F32)
            for tx in range(4):
                piece = jnp.concatenate([chunk[tx * STEP : (tx + 1) * STEP], pad], axis=0)
                out_ref[o, tx, hhi * SLOT : (hhi + 1) * SLOT, :] = piece.astype(BF16)


def row_mask(half, dims, axis):
    def split(value, size):
        whole = jnp.floor((value + 0.5) * (1.0 / size))
        return whole, value - whole * size

    position = lax.broadcasted_iota(jnp.int32, dims, axis).astype(F32)
    group, inside = split(position, BLOCK)
    thi, s = split(group, Z)
    tx, i = split(inside, STEP)
    row = s * (8 * ROWS) + (thi * 4 + tx) * ROWS + (i + (half * HALF).astype(F32))
    return jnp.where((i < HALF - 0.5) & (row < TILE - 0.5), 1.0, 0.0).astype(F32)


def columns(rows):
    return jnp.concatenate([rows[:, g * HD : (g + 1) * HD].astype(F32).T for g in range(4)], axis=1)


def stacked(rows):
    return jnp.concatenate([rows[:, g * HD : (g + 1) * HD] for g in range(4)], axis=0)


def seen_row(ids_ref, count_ref, visible_ref, j):
    y, core, z = ids_ref[0], ids_ref[1], ids_ref[2]
    conv = jnp.int32(CONV_OF[0])
    for i in range(1, Z):
        conv = jnp.where(z == i, CONV_OF[i], conv)
    source = ((y - j) & 3) * 2 + core
    shift = jnp.int32(0)
    for i in range(1, 8):
        shift = jnp.where(source == i, SHIFT[i], shift)
    block = (z + shift) & 7
    seen = jnp.minimum(visible_ref[pl.ds(conv * 8 + block, 1), :], count_ref[conv])
    seen = jnp.where(seen > (y >> 1), 1.0, 0.0).astype(F32)
    return jnp.concatenate([seen] * 4, axis=1)


def weights_of(keys_s, q_t):
    return jnp.exp2(dot(keys_s[...], q_t) * SCALE_LOG2)


def load_pair(ids_ref, mine_ref, other_ref, keys_s, values_s):
    core = ids_ref[1]

    @pl.when(core == 0)
    def _():
        keys_s[...] = mine_ref[...]
        values_s[...] = other_ref[...]

    @pl.when(core != 0)
    def _():
        keys_s[...] = other_ref[...]
        values_s[...] = mine_ref[...]

    return row_mask(ids_ref[0] & 1, (MID, HD), 0)


def thirds(value):
    high = value.astype(BF16).astype(F32)
    middle = (value - high).astype(BF16).astype(F32)
    return [high, middle, value - high - middle]


def forward(ids_ref, count_ref, visible_ref, mine_ref, other_ref, q0, q1, q2, q3, mixed_ref, keys_s, values_s, turned_s):
    y = ids_ref[0]
    ok = load_pair(ids_ref, mine_ref, other_ref, keys_s, values_s)
    keys_s[...] = (keys_s[...].astype(F32) * ok).astype(BF16)
    turned_s[0:HD, :] = (values_s[...].astype(F32) * ok).T.astype(BF16)
    turned_s[HD:, :] = row_mask(ids_ref[0] & 1, (16, MID), 1).astype(BF16)
    rows = []
    for j, q in enumerate((q0, q1, q2, q3)):
        q_t = columns(q[0:128, :]).astype(BF16)
        o_t = columns(q[128:256, :])
        acc = dot(turned_s[...], weights_of(keys_s, q_t).astype(BF16)) * seen_row(ids_ref, count_ref, visible_ref, j)
        mixed_ref[(y - j) & 3, 0:HD, :] = acc[:HD].astype(BF16)
        rows += thirds(acc[HD : HD + 1]) + thirds(jnp.sum(acc[:HD] * o_t, axis=0, keepdims=True))
    rows = jnp.concatenate(rows + [jnp.zeros((MIXED - HD - 24, 512), F32)], axis=0).astype(BF16)
    for to in range(Y):
        mixed_ref[to, HD:, :] = rows


def all_sums(ids_ref, mixed_ref):
    sums = [[jnp.zeros((1, 512), F32)] * 2 for _ in range(Y)]
    for k in range(Y):
        rows = mixed_ref[(ids_ref[0] - k) & 3, HD:, :].astype(F32)
        for j in range(Y):
            at = 6 * ((j - k) & 3)
            for i in range(2):
                first = at + 3 * i
                sums[j][i] = sums[j][i] + (rows[first : first + 1] + rows[first + 1 : first + 2] + rows[first + 2 : first + 3])
    found = []
    for total, product in sums:
        safe = jnp.where(total > 0, total, 1.0)
        found.append((1.0 / safe, product / safe))
    return found


def backward(
    ids_ref, count_ref, visible_ref, mine_ref, other_ref, q0, q1, q2, q3, mixed_ref,
    r0, r1, r2, r3, keep_ref, send_ref, keys_s, values_s, turned_s, dk_s, dv_s,
):
    ok = load_pair(ids_ref, mine_ref, other_ref, keys_s, values_s)
    masked = keys_s[...].astype(F32) * ok
    keys_s[...] = masked.astype(BF16)
    turned_s[...] = masked.T.astype(BF16)
    dk_s[...] = jnp.zeros((MID, HD), F32)
    dv_s[...] = jnp.zeros((MID, HD), F32)
    found = all_sums(ids_ref, mixed_ref)
    for j, (q, r) in enumerate(((q0, r0), (q1, r1), (q2, r2), (q3, r3))):
        q_t = columns(q[0:128, :]).astype(BF16)
        o_t = columns(q[128:256, :]).astype(BF16)
        inverse, delta = found[j]
        inverse = inverse * seen_row(ids_ref, count_ref, visible_ref, j)
        prob = weights_of(keys_s, q_t) * inverse
        d_score = (prob * (dot(values_s[...], o_t) - delta)).astype(BF16)
        dk_s[...] += dot(d_score, stacked(q[0:128, :]))
        dv_s[...] += dot(prob.astype(BF16), stacked(q[128:256, :]))
        r[...] = (dot(turned_s[...], d_score) * SCALE).astype(BF16)
    core = ids_ref[1]

    @pl.when(core == 0)
    def _():
        keep_ref[...] = dk_s[...] * (ok * SCALE)
        send_ref[...] = (dv_s[...] * ok).astype(BF16)

    @pl.when(core != 0)
    def _():
        keep_ref[...] = dv_s[...] * ok
        send_ref[...] = (dk_s[...] * (ok * SCALE)).astype(BF16)


def finish_attended(ids_ref, gate_ref, mixed_ref, out_ref):
    acc = mixed_ref[0, 0:HD, :].astype(F32)
    for i in range(1, Y):
        acc = acc + mixed_ref[i, 0:HD, :].astype(F32)
    acc = acc * all_sums(ids_ref, mixed_ref)[0][0]
    gate = gate_value(gate_ref)
    for g in range(4):
        lanes = slice(g * HD, (g + 1) * HD)
        out_ref[:, lanes] = (acc[:, lanes].T * gate).astype(BF16)


def sum_queries(r0, r1, r2, r3, out_ref):
    dq = r0[...].astype(F32) + r1[...].astype(F32) + r2[...].astype(F32) + r3[...].astype(F32)
    for g in range(4):
        lanes = slice(g * HD, (g + 1) * HD)
        out_ref[:, lanes] = dq[:, lanes].T.astype(BF16)


def norm_back(x, d_normed, gain):
    mean_square = jnp.mean(x * x, axis=-1, keepdims=True)
    inverse = lax.rsqrt(mean_square + EPSILON)
    scaled = d_normed * gain
    dots = jnp.mean(x * scaled, axis=-1, keepdims=True)
    return inverse * scaled - x * (inverse * inverse * inverse * dots)


def finish_queries(queries_ref, got_ref, gains_ref, out_ref):
    gain = gains_ref[0:1]
    for g in range(4):
        lanes = slice(g * HD, (g + 1) * HD)
        x = queries_ref[0, :, lanes].astype(F32)
        out_ref[0, :, lanes] = norm_back(x, got_ref[:, lanes].astype(F32), gain).astype(BF16)


def finish_keys(keys_ref, got_ref, gains_ref, dk_ref, dv_ref):
    gain = gains_ref[1:2]
    for head in range(8):
        hhi, hx = divmod(head, 4)
        lanes = slice(head * HD, (head + 1) * HD)

        def rows(n, kv):
            halves = [got_ref[(n * 2 + half) * 2 + kv, hx, hhi * SLOT : (hhi + 1) * SLOT, :].astype(F32) for half in range(2)]
            return jnp.concatenate([piece[:HALF] for piece in halves], axis=0)

        grads = [norm_back(keys_ref[n, :, lanes].astype(F32), rows(n, 0), gain) for n in range(2)]
        dk_ref[:, :, lanes] = jnp.stack(grads, axis=1).astype(BF16)
        dv_ref[:, :, lanes] = jnp.stack([rows(n, 1) for n in range(2)], axis=1).astype(BF16)


def exchange(value, axes):
    return lax.all_to_all(value, axes, split_axis=0, concat_axis=0, tiled=True)


def rotated(value, k):
    return lax.ppermute(value, "y", [(i, (i + k) % Y) for i in range(Y)])


def swapped(value):
    return lax.ppermute(value, "core", [(0, 1), (1, 0)])


TO_PLANE = [(c * 8 + (z + SHIFT[i]) % 8, i * 8 + z) for i in range(8) for z, c in enumerate(CONV_OF)]
FROM_PLANE = [(b, a) for a, b in TO_PLANE]
PLANES = ("y", "core", "seq")


def shards(queries, keys, values, q_gain, k_gain, gate, tile_count, tile_owner, visible, d_out):
    y, core, z = lax.axis_index("y"), lax.axis_index("core"), lax.axis_index("seq")
    ids = jnp.stack([y, core, z]).astype(jnp.int32)
    q_gain = q_gain.reshape(1, HD)
    k_gain = k_gain.reshape(1, HD)
    owner = lax.dynamic_index_in_dim(tile_owner, y // 2, 1, keepdims=False)
    seen = visible.reshape(64, 128)

    buffers = [pltpu.VMEM((128, 512), BF16), pltpu.VMEM((128, 512), BF16), pltpu.SemaphoreType.DMA((4,))]
    packed, gains = call(
        pack_queries,
        [shape((256, 512), BF16), shape((2, HD), F32)],
        gate, queries, d_out, q_gain, k_gain,
        smem=1, hbm=4, scratch=buffers, limit=60 << 20,
    )
    q0 = lax.ppermute(packed, PLANES, TO_PLANE)
    (packed_kv,) = call(pack_keys, [shape((8, 4, 32, HD), BF16)], keys, values, gains)
    got = exchange(packed_kv.reshape(32, 32, HD), ("y", "core", "x"))
    got, q0 = lax.optimization_barrier((got, q0))
    (chosen,) = call(choose_tiles, [shape((2, 8, BLOCK, HD), BF16)], owner, got.reshape(8, 4, 32, HD), smem=1)
    mine = exchange(chosen.reshape(16, BLOCK, HD), ("zhi", "seq")).reshape(MID, HD)
    q1, q2, q3 = rotated(q0, 1), rotated(q0, 2), rotated(q0, 3)
    other = swapped(mine)

    pair = [pltpu.VMEM((MID, HD), BF16), pltpu.VMEM((MID, HD), BF16)]
    gradients = [pltpu.VMEM((MID, HD), F32), pltpu.VMEM((MID, HD), F32)]
    (mixed,) = call(
        forward,
        [shape((Y, MIXED, 512), BF16)],
        ids, tile_count, seen, mine, other, q0, q1, q2, q3,
        smem=2, scratch=pair + [pltpu.VMEM((HD + 16, MID), BF16)], flops=2 * 2 * 2048 * MID * HD, limit=32 << 20,
    )
    mixed = exchange(mixed, "y")
    r0, r1, r2, r3, keep, send = call(
        backward,
        [shape((HD, 512), BF16)] * 4 + [shape((MID, HD), F32), shape((MID, HD), BF16)],
        ids, tile_count, seen, mine, other, q0, q1, q2, q3, mixed,
        smem=2, scratch=pair + [pltpu.VMEM((HD, MID), BF16)] + gradients, flops=5 * 2 * 2048 * MID * HD, limit=32 << 20,
    )

    grads = (keep + swapped(send).astype(F32)).astype(BF16)
    back = exchange(grads.reshape(16, BLOCK, HD), ("zhi", "seq"))
    (attended,) = call(finish_attended, [shape((128, 512), BF16)], ids, gate, mixed, smem=2)
    attended = lax.ppermute(attended, PLANES, FROM_PLANE)
    r1, r2, r3 = rotated(r1, 3), rotated(r2, 2), rotated(r3, 1)
    back, attended = lax.optimization_barrier((back, attended))
    (placed,) = call(return_tiles, [shape((8, 4, 32, HD), BF16)], owner, back.reshape(2, 8, BLOCK, HD), smem=1)
    home = exchange(placed.reshape(32, 32, HD), ("y", "core", "x")).reshape(8, 4, 32, HD)
    r1, r2, r3, placed = lax.optimization_barrier((r1, r2, r3, placed))
    (d_normed,) = call(sum_queries, [shape((128, 512), BF16)], r0, r1, r2, r3)
    d_normed = lax.ppermute(d_normed, PLANES, FROM_PLANE)
    pairs = shape((ROWS, 2, 8 * HD), BF16)
    d_keys, d_values = call(finish_keys, [pairs, pairs], keys, home, gains, flops=20_000_000_000)
    (d_queries,) = call(finish_queries, [shape(queries.shape, BF16)], queries, d_normed, gains)
    return (attended[None], d_queries, d_keys.transpose(1, 0, 2), d_values.transpose(1, 0, 2))


def solution(mesh):
    parts = Mesh(mesh.devices.reshape(Y, CORE, Z, 2, 4), ("y", "core", "seq", "zhi", "x"))
    conv, tensor = ("y", "core"), ("zhi", "x")
    tokens = P(conv, "seq", tensor)
    rows = P(conv, ("seq", "zhi", "x"), None)
    in_specs = (tokens, rows, rows, P(), P(), P(), P(), P(), P(), tokens)
    out_specs = (tokens, tokens, rows, rows)
    return jax.shard_map(shards, mesh=parts, in_specs=in_specs, out_specs=out_specs, check_vma=False)
```

```python
import math

import jax
import jax.numpy as jnp
from jax import lax
from jax.experimental import pallas as pl
from jax.experimental.pallas import tpu as pltpu
from jax.sharding import Mesh, PartitionSpec as P

HD = 128
TILE = 1601
ROWS = 26
HALF = 13
SLOT = 16
STEP = 14
EPSILON = 1e-05
SCALE = 1.0 / math.sqrt(HD)
SCALE_LOG2 = SCALE / math.log(2.0)
F32 = jnp.float32
HEAVY = 20_000_000_000
BF16 = jnp.bfloat16

Y, CORE, Z, N_O, N_C = 4, 2, 8, 8, 8
PLANE_OF = (0, 7, 1, 6, 2, 5, 3, 4)
CONV_OF = tuple(PLANE_OF.index(z) for z in range(Z))
SHIFT = (0, 4, 1, 3, 2, 6, 5, 7)
BLOCK = 4 * STEP
MID = 2 * Z * BLOCK


def dot(a, b):
    return jnp.dot(a, b, preferred_element_type=F32)


def call(kernel, outs, *args, smem=0, hbm=0, scratch=(), flops=0, limit=8 << 20):
    specs = [pl.BlockSpec(memory_space=pltpu.SMEM)] * smem
    specs += [pl.BlockSpec(memory_space=pltpu.HBM)] * hbm
    specs += [pl.BlockSpec(memory_space=pltpu.VMEM)] * (len(args) - smem - hbm)
    size = sum(a.size * a.dtype.itemsize for a in args) + sum(o.size * o.dtype.itemsize for o in outs)
    return pl.pallas_call(
        kernel,
        out_shape=outs,
        in_specs=specs,
        out_specs=[pl.BlockSpec(memory_space=pltpu.VMEM)] * len(outs),
        scratch_shapes=list(scratch),
        cost_estimate=pl.CostEstimate(flops=flops, bytes_accessed=size, transcendentals=0),
        compiler_params=pltpu.CompilerParams(vmem_limit_bytes=limit),
    )(*args)


def shape(dims, dtype):
    return jax.ShapeDtypeStruct(dims, dtype)


def gate_value(gate_ref):
    return jnp.tanh(jnp.full((1, HD), gate_ref[0], F32))


def pack_queries(gate_ref, queries_ref, d_out_ref, gain_ref, out_ref, x_s, d_s, gain_s, sems):
    copies = [
        pltpu.make_async_copy(source, target, sems.at[i])
        for i, (source, target) in enumerate(
            ((queries_ref.at[0], x_s), (d_out_ref.at[0], d_s), (gain_ref, gain_s))
        )
    ]
    for copy in copies:
        copy.start()
    gate = gate_value(gate_ref)
    for copy in copies:
        copy.wait()
    gain = gain_s[...]
    for g in range(4):
        lanes = slice(g * HD, (g + 1) * HD)
        x = x_s[:, lanes].astype(F32)
        mean_square = jnp.mean(x * x, axis=-1, keepdims=True)
        out_ref[0:128, lanes] = (x * lax.rsqrt(mean_square + EPSILON) * gain).astype(BF16)
        out_ref[128:256, lanes] = (gate * d_s[:, lanes].astype(F32)).astype(BF16)


def turn(packed_ref, out_ref):
    for g in range(4):
        lanes = slice(g * HD, (g + 1) * HD)
        for rows in (slice(0, 128), slice(128, 256)):
            out_ref[rows, lanes] = packed_ref[rows, lanes].astype(F32).T.astype(BF16)


def pack_keys(keys_ref, values_ref, gain_ref, out_ref):
    gain = gain_ref[...]
    for n in range(2):
        for head in range(8):
            hhi, hx = divmod(head, 4)
            lanes = slice(head * HD, (head + 1) * HD)
            x = keys_ref[n, :, lanes].astype(F32)
            mean_square = jnp.mean(x * x, axis=-1, keepdims=True)
            normed = x * lax.rsqrt(mean_square + EPSILON) * gain
            pad = jnp.zeros((SLOT - HALF, HD), F32)
            for kv, rows in ((0, normed), (1, values_ref[n, :, lanes].astype(F32))):
                for half in range(2):
                    at = (n * 2 + half) * 2 + kv
                    piece = jnp.concatenate([rows[half * HALF : (half + 1) * HALF], pad], axis=0)
                    out_ref[at, hx, hhi * SLOT : (hhi + 1) * SLOT, :] = piece.astype(BF16)


def choose_tiles(owner_ref, got_ref, out_ref):
    for z in range(Z):
        o = jnp.maximum(owner_ref[CONV_OF[z]], 0)
        chunk = got_ref[o].astype(F32)
        for hhi in range(2):
            pieces = [chunk[tx, hhi * SLOT : hhi * SLOT + STEP, :] for tx in range(4)]
            out_ref[hhi, z] = jnp.concatenate(pieces, axis=0).astype(BF16)


def return_tiles(owner_ref, got_ref, out_ref):
    for o in range(N_O):
        found = jnp.int32(-1)
        for c in range(N_C):
            found = jnp.where(owner_ref[c] == o, PLANE_OF[c], found)
        at = jnp.maximum(found, 0)
        for hhi in range(2):
            chunk = jnp.where(found >= 0, got_ref[hhi, at].astype(F32), 0.0)
            pad = jnp.zeros((SLOT - STEP, HD), F32)
            for tx in range(4):
                piece = jnp.concatenate([chunk[tx * STEP : (tx + 1) * STEP], pad], axis=0)
                out_ref[o, tx, hhi * SLOT : (hhi + 1) * SLOT, :] = piece.astype(BF16)


def row_mask(half, dims, axis):
    def split(value, size):
        whole = jnp.floor((value + 0.5) * (1.0 / size))
        return whole, value - whole * size

    position = lax.broadcasted_iota(jnp.int32, dims, axis).astype(F32)
    group, inside = split(position, BLOCK)
    thi, s = split(group, Z)
    tx, i = split(inside, STEP)
    row = s * (8 * ROWS) + (thi * 4 + tx) * ROWS + (i + (half * HALF).astype(F32))
    return jnp.where((i < HALF - 0.5) & (row < TILE - 0.5), 1.0, 0.0).astype(F32)


def stacked(columns):
    return jnp.concatenate([columns[:, g * HD : (g + 1) * HD].astype(F32).T.astype(BF16) for g in range(4)], axis=0)


def seen_row(ids_ref, count_ref, visible_ref, j):
    y, core, z = ids_ref[0], ids_ref[1], ids_ref[2]
    conv = jnp.where(z < 4, 2 * z, 15 - 2 * z)
    source = ((y - j) & 3) * 2 + core
    shift = jnp.int32(0)
    for i in range(1, 8):
        shift = jnp.where(source == i, SHIFT[i], shift)
    block = (z + shift) & 7
    seen = jnp.minimum(visible_ref[pl.ds(conv * 8 + block, 1), :], count_ref[conv])
    seen = jnp.where(seen > (y >> 1), 1.0, 0.0).astype(F32)
    return jnp.concatenate([seen] * 4, axis=1)


def weights_of(keys_s, q_t):
    return jnp.exp2(dot(keys_s[...], q_t) * SCALE_LOG2)


def load_pair(ids_ref, mine_ref, other_ref, keys_s, values_s):
    core = ids_ref[1]

    @pl.when(core == 0)
    def _():
        keys_s[...] = mine_ref[...]
        values_s[...] = other_ref[...]

    @pl.when(core != 0)
    def _():
        keys_s[...] = other_ref[...]
        values_s[...] = mine_ref[...]

    return row_mask(ids_ref[0] & 1, (MID, HD), 0)


def forward(ids_ref, count_ref, visible_ref, mine_ref, other_ref, q0, q1, q2, q3, acc_ref, sums_ref, keys_s, values_s, turned_s, q_s):
    ok = load_pair(ids_ref, mine_ref, other_ref, keys_s, values_s)
    keys_s[...] = (keys_s[...].astype(F32) * ok).astype(BF16)
    turned_s[0:HD, :] = (values_s[...].astype(F32) * ok).T.astype(BF16)
    turned_s[HD:, :] = row_mask(ids_ref[0] & 1, (16, MID), 1).astype(BF16)
    for j, q in enumerate((q0, q1, q2, q3)):
        q_s[j] = q[...]

    def block(j, carry):
        q_t = q_s[j, 0:128, :]
        o_t = q_s[j, 128:256, :].astype(F32)
        acc = dot(turned_s[...], weights_of(keys_s, q_t).astype(BF16))
        acc = acc * seen_row(ids_ref, count_ref, visible_ref, j)
        both = jnp.concatenate([acc[HD : HD + 1], jnp.sum(acc[:HD] * o_t, axis=0, keepdims=True)], axis=0)
        for to in range(Y):
            sums_ref[to, j] = both
        acc_ref[j] = acc[:HD]
        return carry

    lax.fori_loop(0, Y, block, 0, unroll=True)


def all_sums(ids_ref, sums_ref, j):
    y = ids_ref[0]
    both = sums_ref[y, j]
    for k in range(1, Y):
        both = both + sums_ref[(y - k) & 3, (j - k) & 3]
    total = both[0:1]
    safe = jnp.where(total > 0, total, 1.0)
    return 1.0 / safe, both[1:2] / safe


def backward(
    ids_ref, count_ref, visible_ref, mine_ref, other_ref, q0, q1, q2, q3, acc_ref, sums_ref,
    r0, r1, r2, r3, keep_ref, send_ref, keys_s, values_s, turned_s, q_s, dk_s, dv_s,
):
    ok = load_pair(ids_ref, mine_ref, other_ref, keys_s, values_s)
    masked = keys_s[...].astype(F32) * ok
    keys_s[...] = masked.astype(BF16)
    turned_s[...] = masked.T.astype(BF16)
    dk_s[...] = jnp.zeros((MID, HD), F32)
    dv_s[...] = jnp.zeros((MID, HD), F32)
    for j, q in enumerate((q0, q1, q2, q3)):
        q_s[j] = q[...]

    def block(j, carry):
        q_t = q_s[j, 0:128, :]
        o_t = q_s[j, 128:256, :]
        q_rows = stacked(q_t)
        o_rows = stacked(o_t)
        inverse, delta = all_sums(ids_ref, sums_ref, j)
        acc = (acc_ref[j] * inverse).astype(BF16)
        inverse = inverse * seen_row(ids_ref, count_ref, visible_ref, j)
        prob = weights_of(keys_s, q_t) * inverse
        d_score = (prob * (dot(values_s[...], o_t) - delta)).astype(BF16)
        dk_s[...] += dot(d_score, q_rows)
        dv_s[...] += dot(prob.astype(BF16), o_rows)
        dq = dot(turned_s[...], d_score)
        q_s[j] = jnp.concatenate([acc, (dq * SCALE).astype(BF16)], axis=0)
        return carry

    lax.fori_loop(0, Y, block, 0, unroll=2)
    for j, r in enumerate((r0, r1, r2, r3)):
        r[...] = q_s[j]
    core = ids_ref[1]

    @pl.when(core == 0)
    def _():
        keep_ref[...] = dk_s[...] * (ok * SCALE)
        send_ref[...] = (dv_s[...] * ok).astype(BF16)

    @pl.when(core != 0)
    def _():
        keep_ref[...] = dv_s[...] * ok
        send_ref[...] = (dk_s[...] * (ok * SCALE)).astype(BF16)


def sum_tokens(gate_ref, r0, r1, r2, r3, out_ref):
    gate = gate_value(gate_ref)
    both = r0[...].astype(F32) + r1[...].astype(F32) + r2[...].astype(F32) + r3[...].astype(F32)
    for g in range(4):
        lanes = slice(g * HD, (g + 1) * HD)
        out_ref[0:128, lanes] = (both[0:128, lanes].T * gate).astype(BF16)
        out_ref[128:256, lanes] = both[128:256, lanes].T.astype(BF16)


def norm_back(x, d_normed, gain):
    mean_square = jnp.mean(x * x, axis=-1, keepdims=True)
    inverse = lax.rsqrt(mean_square + EPSILON)
    scaled = d_normed * gain
    dots = jnp.mean(x * scaled, axis=-1, keepdims=True)
    return inverse * scaled - x * (inverse * inverse * inverse * dots)


def finish_queries(queries_ref, got_ref, gain_ref, attended_ref, out_ref):
    gain = gain_ref[...]
    attended_ref[0] = got_ref[0:128, :]
    for g in range(4):
        lanes = slice(g * HD, (g + 1) * HD)
        x = queries_ref[0, :, lanes].astype(F32)
        out_ref[0, :, lanes] = norm_back(x, got_ref[128:256, lanes].astype(F32), gain).astype(BF16)


def finish_keys(keys_ref, got_ref, gain_ref, dk_ref, dv_ref):
    gain = gain_ref[...]
    for n in range(2):
        for head in range(8):
            hhi, hx = divmod(head, 4)
            lanes = slice(head * HD, (head + 1) * HD)
            x = keys_ref[n, :, lanes].astype(F32)

            def rows(kv):
                halves = [got_ref[(n * 2 + half) * 2 + kv, hx, hhi * SLOT : (hhi + 1) * SLOT, :].astype(F32) for half in range(2)]
                return jnp.concatenate([piece[:HALF] for piece in halves], axis=0)

            dk_ref[n, :, lanes] = norm_back(x, rows(0), gain).astype(BF16)
            dv_ref[n, :, lanes] = rows(1).astype(BF16)


def exchange(value, axes):
    return lax.all_to_all(value, axes, split_axis=0, concat_axis=0, tiled=True)


def rotated(value, k):
    return lax.ppermute(value, "y", [(i, (i + k) % Y) for i in range(Y)])


def swapped(value):
    return lax.ppermute(value, "core", [(0, 1), (1, 0)])


TO_PLANE = [(c * 8 + (z + SHIFT[i]) % 8, i * 8 + z) for i in range(8) for z, c in enumerate(CONV_OF)]
FROM_PLANE = [(b, a) for a, b in TO_PLANE]
PLANES = ("y", "core", "seq")


def shards(queries, keys, values, q_gain, k_gain, gate, tile_count, tile_owner, visible, d_out):
    y, core, z = lax.axis_index("y"), lax.axis_index("core"), lax.axis_index("seq")
    ids = jnp.stack([y, core, z]).astype(jnp.int32)
    q_gain = q_gain.reshape(1, HD)
    k_gain = k_gain.reshape(1, HD)
    owner = lax.dynamic_index_in_dim(tile_owner, y // 2, 1, keepdims=False)
    seen = visible.reshape(64, 128)

    (packed_kv,) = call(pack_keys, [shape((8, 4, 32, HD), BF16)], keys, values, k_gain)
    packed_kv, queries = lax.optimization_barrier((packed_kv, queries))
    buffers = [pltpu.VMEM((128, 512), BF16), pltpu.VMEM((128, 512), BF16), pltpu.VMEM((1, HD), F32), pltpu.SemaphoreType.DMA((3,))]
    (packed,) = call(
        pack_queries,
        [shape((256, 512), BF16)],
        gate, queries, d_out, q_gain,
        smem=1, hbm=3, scratch=buffers, limit=60 << 20,
    )
    (q0,) = call(turn, [shape((256, 512), BF16)], lax.ppermute(packed, PLANES, TO_PLANE), flops=HEAVY)
    got = exchange(packed_kv.reshape(32, 32, HD), ("y", "core", "x"))
    (chosen,) = call(choose_tiles, [shape((2, 8, BLOCK, HD), BF16)], owner, got.reshape(8, 4, 32, HD), smem=1)
    mine = exchange(chosen.reshape(16, BLOCK, HD), ("zhi", "seq")).reshape(MID, HD)
    q1, q2, q3 = rotated(q0, 1), rotated(q0, 2), rotated(q0, 3)
    other = swapped(mine)

    pair = [pltpu.VMEM((MID, HD), BF16), pltpu.VMEM((MID, HD), BF16)]
    tokens = pltpu.VMEM((Y, 256, 512), BF16)
    gradients = [pltpu.VMEM((MID, HD), F32), pltpu.VMEM((MID, HD), F32)]
    acc, sums = call(
        forward,
        [shape((Y, HD, 512), F32), shape((Y, Y, 2, 512), F32)],
        ids, tile_count, seen, mine, other, q0, q1, q2, q3,
        smem=2, scratch=pair + [pltpu.VMEM((HD + 16, MID), BF16), tokens], flops=2 * 2 * 2048 * MID * HD, limit=32 << 20,
    )
    sums = exchange(sums, "y")
    r0, r1, r2, r3, keep, send = call(
        backward,
        [shape((256, 512), BF16)] * 4 + [shape((MID, HD), F32), shape((MID, HD), BF16)],
        ids, tile_count, seen, mine, other, q0, q1, q2, q3, acc, sums,
        smem=2, scratch=pair + [pltpu.VMEM((HD, MID), BF16), tokens] + gradients, flops=5 * 2 * 2048 * MID * HD, limit=32 << 20,
    )

    grads = (keep + swapped(send).astype(F32)).astype(BF16)
    back = exchange(grads.reshape(16, BLOCK, HD), ("zhi", "seq"))
    r1, r2, r3 = rotated(r1, 3), rotated(r2, 2), rotated(r3, 1)
    (placed,) = call(return_tiles, [shape((8, 4, 32, HD), BF16)], owner, back.reshape(2, 8, BLOCK, HD), smem=1)
    home = exchange(placed.reshape(32, 32, HD), ("y", "core", "x")).reshape(8, 4, 32, HD)
    r1, r2, r3, placed = lax.optimization_barrier((r1, r2, r3, placed))
    (summed,) = call(sum_tokens, [shape((256, 512), BF16)], gate, r0, r1, r2, r3, smem=1)
    summed = lax.ppermute(summed, PLANES, FROM_PLANE)
    d_keys, d_values = call(finish_keys, [shape(keys.shape, BF16), shape(values.shape, BF16)], keys, home, k_gain, flops=HEAVY)
    attended, d_queries = call(finish_queries, [shape(queries.shape, BF16)] * 2, queries, summed, q_gain)
    return (attended, d_queries, d_keys, d_values)


def solution(mesh):
    parts = Mesh(mesh.devices.reshape(Y, CORE, Z, 2, 4), ("y", "core", "seq", "zhi", "x"))
    conv, tensor = ("y", "core"), ("zhi", "x")
    tokens = P(conv, "seq", tensor)
    rows = P(conv, ("seq", "zhi", "x"), None)
    in_specs = (tokens, rows, rows, P(), P(), P(), P(), P(), P(), tokens)
    out_specs = (tokens, tokens, rows, rows)
    return jax.shard_map(shards, mesh=parts, in_specs=in_specs, out_specs=out_specs, check_vma=False)
```

```python
import math

import jax
import jax.numpy as jnp
from jax import lax
from jax.experimental import pallas as pl
from jax.experimental.pallas import tpu as pltpu
from jax.sharding import Mesh, PartitionSpec as P

HD = 128
TILE = 1601
ROWS = 26
HALF = 13
SLOT = 16
STEP = 14
EPSILON = 1e-05
SCALE = 1.0 / math.sqrt(HD)
SCALE_LOG2 = SCALE / math.log(2.0)
F32 = jnp.float32
HEAVY = 20_000_000_000
BF16 = jnp.bfloat16

Y, CORE, Z, N_O, N_C = 4, 2, 8, 8, 8
PLANE_OF = (0, 7, 1, 6, 2, 5, 3, 4)
CONV_OF = tuple(PLANE_OF.index(z) for z in range(Z))
SHIFT = (0, 4, 1, 3, 2, 6, 5, 7)
BLOCK = 4 * STEP
MID = 2 * Z * BLOCK


def dot(a, b):
    return jnp.dot(a, b, preferred_element_type=F32)


def call(kernel, outs, *args, smem=0, hbm=0, scratch=(), flops=0, limit=8 << 20):
    specs = [pl.BlockSpec(memory_space=pltpu.SMEM)] * smem
    specs += [pl.BlockSpec(memory_space=pltpu.HBM)] * hbm
    specs += [pl.BlockSpec(memory_space=pltpu.VMEM)] * (len(args) - smem - hbm)
    size = sum(a.size * a.dtype.itemsize for a in args) + sum(o.size * o.dtype.itemsize for o in outs)
    return pl.pallas_call(
        kernel,
        out_shape=outs,
        in_specs=specs,
        out_specs=[pl.BlockSpec(memory_space=pltpu.VMEM)] * len(outs),
        scratch_shapes=list(scratch),
        cost_estimate=pl.CostEstimate(flops=flops, bytes_accessed=size, transcendentals=0),
        compiler_params=pltpu.CompilerParams(vmem_limit_bytes=limit),
    )(*args)


def shape(dims, dtype):
    return jax.ShapeDtypeStruct(dims, dtype)


def gate_value(gate_ref):
    return jnp.tanh(jnp.full((1, HD), gate_ref[0], F32))


def pack_queries(gate_ref, queries_ref, d_out_ref, gain_ref, out_ref, x_s, d_s, gain_s, sems):
    copies = [
        pltpu.make_async_copy(source, target, sems.at[i])
        for i, (source, target) in enumerate(
            ((queries_ref.at[0], x_s), (d_out_ref.at[0], d_s), (gain_ref, gain_s))
        )
    ]
    for copy in copies:
        copy.start()
    gate = gate_value(gate_ref)
    for copy in copies:
        copy.wait()
    gain = gain_s[...]
    for g in range(4):
        lanes = slice(g * HD, (g + 1) * HD)
        x = x_s[:, lanes].astype(F32)
        mean_square = jnp.mean(x * x, axis=-1, keepdims=True)
        out_ref[0:128, lanes] = (x * lax.rsqrt(mean_square + EPSILON) * gain).astype(BF16)
        out_ref[128:256, lanes] = (gate * d_s[:, lanes].astype(F32)).astype(BF16)


def turn(packed_ref, out_ref):
    for g in range(4):
        lanes = slice(g * HD, (g + 1) * HD)
        for rows in (slice(0, 128), slice(128, 256)):
            out_ref[rows, lanes] = packed_ref[rows, lanes].astype(F32).T.astype(BF16)


def owners_of(ids_ref, table_ref, *rest):
    for c in range(N_C):
        rest[-1][c] = jnp.where(ids_ref[0] >= 2, table_ref[c, 1], table_ref[c, 0])


def pack_keys(keys_ref, values_ref, gain_ref, out_ref):
    gain = gain_ref[...]
    for n in range(2):
        for head in range(8):
            hhi, hx = divmod(head, 4)
            lanes = slice(head * HD, (head + 1) * HD)
            x = keys_ref[n, :, lanes].astype(F32)
            mean_square = jnp.mean(x * x, axis=-1, keepdims=True)
            normed = x * lax.rsqrt(mean_square + EPSILON) * gain
            pad = jnp.zeros((SLOT - HALF, HD), F32)
            for kv, rows in ((0, normed), (1, values_ref[n, :, lanes].astype(F32))):
                for half in range(2):
                    at = (n * 2 + half) * 2 + kv
                    piece = jnp.concatenate([rows[half * HALF : (half + 1) * HALF], pad], axis=0)
                    out_ref[at, hx, hhi * SLOT : (hhi + 1) * SLOT, :] = piece.astype(BF16)


def choose_tiles(owner_ref, got_ref, out_ref):
    for z in range(Z):
        o = jnp.maximum(owner_ref[CONV_OF[z]], 0)
        chunk = got_ref[o].astype(F32)
        for hhi in range(2):
            pieces = [chunk[tx, hhi * SLOT : hhi * SLOT + STEP, :] for tx in range(4)]
            out_ref[hhi, z] = jnp.concatenate(pieces, axis=0).astype(BF16)


def return_tiles(owner_ref, got_ref, out_ref):
    for o in range(N_O):
        found = jnp.int32(-1)
        for c in range(N_C):
            found = jnp.where(owner_ref[c] == o, PLANE_OF[c], found)
        at = jnp.maximum(found, 0)
        for hhi in range(2):
            chunk = jnp.where(found >= 0, got_ref[hhi, at].astype(F32), 0.0)
            pad = jnp.zeros((SLOT - STEP, HD), F32)
            for tx in range(4):
                piece = jnp.concatenate([chunk[tx * STEP : (tx + 1) * STEP], pad], axis=0)
                out_ref[o, tx, hhi * SLOT : (hhi + 1) * SLOT, :] = piece.astype(BF16)


def row_mask(half, dims, axis):
    def split(value, size):
        whole = jnp.floor((value + 0.5) * (1.0 / size))
        return whole, value - whole * size

    position = lax.broadcasted_iota(jnp.int32, dims, axis).astype(F32)
    group, inside = split(position, BLOCK)
    thi, s = split(group, Z)
    tx, i = split(inside, STEP)
    row = s * (8 * ROWS) + (thi * 4 + tx) * ROWS + (i + (half * HALF).astype(F32))
    return jnp.where((i < HALF - 0.5) & (row < TILE - 0.5), 1.0, 0.0).astype(F32)


def stacked(columns):
    return jnp.concatenate([columns[:, g * HD : (g + 1) * HD].astype(F32).T.astype(BF16) for g in range(4)], axis=0)


def seen_row(ids_ref, count_ref, visible_ref, j):
    y, core, z = ids_ref[0], ids_ref[1], ids_ref[2]
    conv = jnp.where(z < 4, 2 * z, 15 - 2 * z)
    source = ((y - j) & 3) * 2 + core
    shift = jnp.int32(0)
    for i in range(1, 8):
        shift = jnp.where(source == i, SHIFT[i], shift)
    block = (z + shift) & 7
    seen = jnp.minimum(visible_ref[pl.ds(conv * 8 + block, 1), :], count_ref[conv])
    seen = jnp.where(seen > (y >> 1), 1.0, 0.0).astype(F32)
    return jnp.concatenate([seen] * 4, axis=1)


def weights_of(keys_s, q_t):
    return jnp.exp2(dot(keys_s[...], q_t) * SCALE_LOG2)


def load_pair(ids_ref, mine_ref, other_ref, keys_s, values_s):
    core = ids_ref[1]

    @pl.when(core == 0)
    def _():
        keys_s[...] = mine_ref[...]
        values_s[...] = other_ref[...]

    @pl.when(core != 0)
    def _():
        keys_s[...] = other_ref[...]
        values_s[...] = mine_ref[...]

    return row_mask(ids_ref[0] & 1, (MID, HD), 0)


def forward(ids_ref, count_ref, visible_ref, mine_ref, other_ref, q0, q1, q2, q3, acc_ref, sums_ref, keys_s, values_s, turned_s, q_s):
    ok = load_pair(ids_ref, mine_ref, other_ref, keys_s, values_s)
    keys_s[...] = (keys_s[...].astype(F32) * ok).astype(BF16)
    turned_s[0:HD, :] = (values_s[...].astype(F32) * ok).T.astype(BF16)
    turned_s[HD:, :] = row_mask(ids_ref[0] & 1, (16, MID), 1).astype(BF16)
    for j, q in enumerate((q0, q1, q2, q3)):
        q_s[j] = q[...]

    def block(j, carry):
        q_t = q_s[j, 0:128, :]
        o_t = q_s[j, 128:256, :].astype(F32)
        acc = dot(turned_s[...], weights_of(keys_s, q_t).astype(BF16))
        acc = acc * seen_row(ids_ref, count_ref, visible_ref, j)
        both = jnp.concatenate([acc[HD : HD + 1], jnp.sum(acc[:HD] * o_t, axis=0, keepdims=True)], axis=0)
        for to in range(Y):
            sums_ref[to, j] = both
        acc_ref[j] = acc[:HD]
        return carry

    lax.fori_loop(0, Y, block, 0, unroll=True)


def all_sums(ids_ref, sums_ref, j):
    y = ids_ref[0]
    both = sums_ref[y, j]
    for k in range(1, Y):
        both = both + sums_ref[(y - k) & 3, (j - k) & 3]
    total = both[0:1]
    safe = jnp.where(total > 0, total, 1.0)
    return 1.0 / safe, both[1:2] / safe


def backward(
    ids_ref, count_ref, visible_ref, mine_ref, other_ref, q0, q1, q2, q3, acc_ref, sums_ref,
    r0, r1, r2, r3, keep_ref, send_ref, keys_s, values_s, turned_s, q_s, dk_s, dv_s,
):
    ok = load_pair(ids_ref, mine_ref, other_ref, keys_s, values_s)
    masked = keys_s[...].astype(F32) * ok
    keys_s[...] = masked.astype(BF16)
    turned_s[...] = masked.T.astype(BF16)
    dk_s[...] = jnp.zeros((MID, HD), F32)
    dv_s[...] = jnp.zeros((MID, HD), F32)
    for j, q in enumerate((q0, q1, q2, q3)):
        q_s[j] = q[...]

    def block(j, carry):
        q_t = q_s[j, 0:128, :]
        o_t = q_s[j, 128:256, :]
        q_rows = stacked(q_t)
        o_rows = stacked(o_t)
        inverse, delta = all_sums(ids_ref, sums_ref, j)
        acc = (acc_ref[j] * inverse).astype(BF16)
        inverse = inverse * seen_row(ids_ref, count_ref, visible_ref, j)
        prob = weights_of(keys_s, q_t) * inverse
        d_score = (prob * (dot(values_s[...], o_t) - delta)).astype(BF16)
        dk_s[...] += dot(d_score, q_rows)
        dv_s[...] += dot(prob.astype(BF16), o_rows)
        dq = dot(turned_s[...], d_score)
        q_s[j] = jnp.concatenate([acc, (dq * SCALE).astype(BF16)], axis=0)
        return carry

    lax.fori_loop(0, Y, block, 0, unroll=2)
    for j, r in enumerate((r0, r1, r2, r3)):
        r[...] = q_s[j]
    core = ids_ref[1]

    @pl.when(core == 0)
    def _():
        keep_ref[...] = dk_s[...] * (ok * SCALE)
        send_ref[...] = (dv_s[...] * ok).astype(BF16)

    @pl.when(core != 0)
    def _():
        keep_ref[...] = dv_s[...] * ok
        send_ref[...] = (dk_s[...] * (ok * SCALE)).astype(BF16)


def sum_tokens(gate_ref, r0, r1, r2, r3, out_ref):
    gate = gate_value(gate_ref)
    both = r0[...].astype(F32) + r1[...].astype(F32) + r2[...].astype(F32) + r3[...].astype(F32)
    for g in range(4):
        lanes = slice(g * HD, (g + 1) * HD)
        out_ref[0:128, lanes] = (both[0:128, lanes].T * gate).astype(BF16)
        out_ref[128:256, lanes] = both[128:256, lanes].T.astype(BF16)


def norm_back(x, d_normed, gain):
    mean_square = jnp.mean(x * x, axis=-1, keepdims=True)
    inverse = lax.rsqrt(mean_square + EPSILON)
    scaled = d_normed * gain
    dots = jnp.mean(x * scaled, axis=-1, keepdims=True)
    return inverse * scaled - x * (inverse * inverse * inverse * dots)


def finish_queries(queries_ref, got_ref, gain_ref, attended_ref, out_ref):
    gain = gain_ref[...]
    attended_ref[0] = got_ref[0:128, :]
    for g in range(4):
        lanes = slice(g * HD, (g + 1) * HD)
        x = queries_ref[0, :, lanes].astype(F32)
        out_ref[0, :, lanes] = norm_back(x, got_ref[128:256, lanes].astype(F32), gain).astype(BF16)


def finish_keys(keys_ref, got_ref, gain_ref, dk_ref, dv_ref):
    gain = gain_ref[...]
    for n in range(2):
        for head in range(8):
            hhi, hx = divmod(head, 4)
            lanes = slice(head * HD, (head + 1) * HD)
            x = keys_ref[n, :, lanes].astype(F32)

            def rows(kv):
                halves = [got_ref[(n * 2 + half) * 2 + kv, hx, hhi * SLOT : (hhi + 1) * SLOT, :].astype(F32) for half in range(2)]
                return jnp.concatenate([piece[:HALF] for piece in halves], axis=0)

            dk_ref[n, :, lanes] = norm_back(x, rows(0), gain).astype(BF16)
            dv_ref[n, :, lanes] = rows(1).astype(BF16)


def exchange(value, axes):
    return lax.all_to_all(value, axes, split_axis=0, concat_axis=0, tiled=True)


def rotated(value, k):
    return lax.ppermute(value, "y", [(i, (i + k) % Y) for i in range(Y)])


def swapped(value):
    return lax.ppermute(value, "core", [(0, 1), (1, 0)])


TO_PLANE = [(c * 8 + (z + SHIFT[i]) % 8, i * 8 + z) for i in range(8) for z, c in enumerate(CONV_OF)]
FROM_PLANE = [(b, a) for a, b in TO_PLANE]
PLANES = ("y", "core", "seq")


def shards(queries, keys, values, q_gain, k_gain, gate, tile_count, tile_owner, visible, d_out):
    y, core, z = lax.axis_index("y"), lax.axis_index("core"), lax.axis_index("seq")
    ids = jnp.stack([y, core, z]).astype(jnp.int32)
    q_gain = q_gain.reshape(1, HD)
    k_gain = k_gain.reshape(1, HD)
    seen = visible.reshape(64, 128)

    (packed_kv,) = call(pack_keys, [shape((8, 4, 32, HD), BF16)], keys, values, k_gain)
    packed_kv, queries = lax.optimization_barrier((packed_kv, queries))
    buffers = [pltpu.VMEM((128, 512), BF16), pltpu.VMEM((128, 512), BF16), pltpu.VMEM((1, HD), F32), pltpu.SemaphoreType.DMA((3,))]
    (packed,) = call(
        pack_queries,
        [shape((256, 512), BF16)],
        gate, queries, d_out, q_gain,
        smem=1, hbm=3, scratch=buffers, limit=60 << 20,
    )
    owner = pl.pallas_call(
        owners_of,
        out_shape=shape((N_C,), jnp.int32),
        in_specs=[pl.BlockSpec(memory_space=pltpu.SMEM)] * 2,
        out_specs=pl.BlockSpec(memory_space=pltpu.SMEM),
        cost_estimate=pl.CostEstimate(flops=HEAVY, bytes_accessed=64, transcendentals=0),
        compiler_params=pltpu.CompilerParams(vmem_limit_bytes=1 << 20),
    )(ids, tile_owner)
    (q0,) = call(turn, [shape((256, 512), BF16)], lax.ppermute(packed, PLANES, TO_PLANE), flops=HEAVY)
    got = exchange(packed_kv.reshape(32, 32, HD), ("y", "core", "x"))
    (chosen,) = call(choose_tiles, [shape((2, 8, BLOCK, HD), BF16)], owner, got.reshape(8, 4, 32, HD), smem=1)
    mine = exchange(chosen.reshape(16, BLOCK, HD), ("zhi", "seq")).reshape(MID, HD)
    q1, q2, q3 = rotated(q0, 1), rotated(q0, 2), rotated(q0, 3)
    other = swapped(mine)

    pair = [pltpu.VMEM((MID, HD), BF16), pltpu.VMEM((MID, HD), BF16)]
    tokens = pltpu.VMEM((Y, 256, 512), BF16)
    gradients = [pltpu.VMEM((MID, HD), F32), pltpu.VMEM((MID, HD), F32)]
    acc, sums = call(
        forward,
        [shape((Y, HD, 512), F32), shape((Y, Y, 2, 512), F32)],
        ids, tile_count, seen, mine, other, q0, q1, q2, q3,
        smem=2, scratch=pair + [pltpu.VMEM((HD + 16, MID), BF16), tokens], flops=2 * 2 * 2048 * MID * HD, limit=32 << 20,
    )
    sums = exchange(sums, "y")
    r0, r1, r2, r3, keep, send = call(
        backward,
        [shape((256, 512), BF16)] * 4 + [shape((MID, HD), F32), shape((MID, HD), BF16)],
        ids, tile_count, seen, mine, other, q0, q1, q2, q3, acc, sums,
        smem=2, scratch=pair + [pltpu.VMEM((HD, MID), BF16), tokens] + gradients, flops=5 * 2 * 2048 * MID * HD, limit=32 << 20,
    )

    grads = (keep + swapped(send).astype(F32)).astype(BF16)
    back = exchange(grads.reshape(16, BLOCK, HD), ("zhi", "seq"))
    r1, r2, r3 = rotated(r1, 3), rotated(r2, 2), rotated(r3, 1)
    (placed,) = call(return_tiles, [shape((8, 4, 32, HD), BF16)], owner, back.reshape(2, 8, BLOCK, HD), smem=1)
    home = exchange(placed.reshape(32, 32, HD), ("y", "core", "x")).reshape(8, 4, 32, HD)
    r1, r2, r3, placed = lax.optimization_barrier((r1, r2, r3, placed))
    (summed,) = call(sum_tokens, [shape((256, 512), BF16)], gate, r0, r1, r2, r3, smem=1)
    summed = lax.ppermute(summed, PLANES, FROM_PLANE)
    d_keys, d_values = call(finish_keys, [shape(keys.shape, BF16), shape(values.shape, BF16)], keys, home, k_gain, flops=HEAVY)
    attended, d_queries = call(finish_queries, [shape(queries.shape, BF16)] * 2, queries, summed, q_gain)
    return (attended, d_queries, d_keys, d_values)


def solution(mesh):
    parts = Mesh(mesh.devices.reshape(Y, CORE, Z, 2, 4), ("y", "core", "seq", "zhi", "x"))
    conv, tensor = ("y", "core"), ("zhi", "x")
    tokens = P(conv, "seq", tensor)
    rows = P(conv, ("seq", "zhi", "x"), None)
    in_specs = (tokens, rows, rows, P(), P(), P(), P(), P(), P(), tokens)
    out_specs = (tokens, tokens, rows, rows)
    return jax.shard_map(shards, mesh=parts, in_specs=in_specs, out_specs=out_specs, check_vma=False)
```

```python
import math

import jax
import jax.numpy as jnp
from jax import lax
from jax.experimental import pallas as pl
from jax.experimental.pallas import tpu as pltpu
from jax.sharding import Mesh, PartitionSpec as P

HD = 128
TILE = 1601
ROWS = 26
HALF = 13
SLOT = 16
STEP = 14
EPSILON = 1e-05
SCALE = 1.0 / math.sqrt(HD)
SCALE_LOG2 = SCALE / math.log(2.0)
F32 = jnp.float32
HEAVY = 20_000_000_000
BF16 = jnp.bfloat16

Y, CORE, Z, N_O, N_C = 4, 2, 8, 8, 8
PLANE_OF = (0, 7, 1, 6, 2, 5, 3, 4)
CONV_OF = tuple(PLANE_OF.index(z) for z in range(Z))
SHIFT = (0, 4, 1, 3, 2, 6, 5, 7)
BLOCK = 4 * STEP
MID = 2 * Z * BLOCK
ALL = 2 * MID
BLOCKS = 2


def dot(a, b):
    return jnp.dot(a, b, preferred_element_type=F32)


def call(kernel, outs, *args, smem=0, hbm=0, scratch=(), flops=0, limit=8 << 20):
    specs = [pl.BlockSpec(memory_space=pltpu.SMEM)] * smem
    specs += [pl.BlockSpec(memory_space=pltpu.HBM)] * hbm
    specs += [pl.BlockSpec(memory_space=pltpu.VMEM)] * (len(args) - smem - hbm)
    size = sum(a.size * a.dtype.itemsize for a in args) + sum(o.size * o.dtype.itemsize for o in outs)
    return pl.pallas_call(
        kernel,
        out_shape=outs,
        in_specs=specs,
        out_specs=[pl.BlockSpec(memory_space=pltpu.VMEM)] * len(outs),
        scratch_shapes=list(scratch),
        cost_estimate=pl.CostEstimate(flops=flops, bytes_accessed=size, transcendentals=0),
        compiler_params=pltpu.CompilerParams(vmem_limit_bytes=limit),
    )(*args)


def shape(dims, dtype):
    return jax.ShapeDtypeStruct(dims, dtype)


def gate_value(gate_ref):
    return jnp.tanh(jnp.full((1, HD), gate_ref[0], F32))


def pack_queries(gate_ref, queries_ref, d_out_ref, gain_ref, out_ref, x_s, d_s, gain_s, sems):
    copies = [
        pltpu.make_async_copy(source, target, sems.at[i])
        for i, (source, target) in enumerate(
            ((queries_ref.at[0], x_s), (d_out_ref.at[0], d_s), (gain_ref, gain_s))
        )
    ]
    for copy in copies:
        copy.start()
    gate = gate_value(gate_ref)
    for copy in copies:
        copy.wait()
    gain = gain_s[...]
    for g in range(4):
        lanes = slice(g * HD, (g + 1) * HD)
        x = x_s[:, lanes].astype(F32)
        mean_square = jnp.mean(x * x, axis=-1, keepdims=True)
        out_ref[0:128, lanes] = (x * lax.rsqrt(mean_square + EPSILON) * gain).astype(BF16)
        out_ref[128:256, lanes] = (gate * d_s[:, lanes].astype(F32)).astype(BF16)


def turn(packed_ref, out_ref):
    for g in range(4):
        lanes = slice(g * HD, (g + 1) * HD)
        for rows in (slice(0, 128), slice(128, 256)):
            out_ref[rows, lanes] = packed_ref[rows, lanes].astype(F32).T.astype(BF16)


def owners_of(ids_ref, table_ref, *rest):
    for c in range(N_C):
        rest[-1][c] = jnp.where(ids_ref[0] >= 2, table_ref[c, 1], table_ref[c, 0])


def pack_keys(keys_ref, values_ref, gain_ref, out_ref):
    gain = gain_ref[...]
    for n in range(2):
        for head in range(8):
            hhi, hx = divmod(head, 4)
            lanes = slice(head * HD, (head + 1) * HD)
            x = keys_ref[n, :, lanes].astype(F32)
            mean_square = jnp.mean(x * x, axis=-1, keepdims=True)
            normed = x * lax.rsqrt(mean_square + EPSILON) * gain
            pad = jnp.zeros((SLOT - HALF, HD), F32)
            for kv, rows in ((0, normed), (1, values_ref[n, :, lanes].astype(F32))):
                for half in range(2):
                    at = (n * 2 + half) * 2 + kv
                    piece = jnp.concatenate([rows[half * HALF : (half + 1) * HALF], pad], axis=0)
                    out_ref[at, hx, hhi * SLOT : (hhi + 1) * SLOT, :] = piece.astype(BF16)


def choose_tiles(owner_ref, got_ref, out_ref):
    for z in range(Z):
        o = jnp.maximum(owner_ref[CONV_OF[z]], 0)
        chunk = got_ref[o].astype(F32)
        for hhi in range(2):
            pieces = [chunk[tx, hhi * SLOT : hhi * SLOT + STEP, :] for tx in range(4)]
            out_ref[hhi, z] = jnp.concatenate(pieces, axis=0).astype(BF16)


def return_tiles(owner_ref, got_ref, out_ref):
    for o in range(N_O):
        found = jnp.int32(-1)
        for c in range(N_C):
            found = jnp.where(owner_ref[c] == o, PLANE_OF[c], found)
        at = jnp.maximum(found, 0)
        for hhi in range(2):
            chunk = jnp.where(found >= 0, got_ref[hhi, at].astype(F32), 0.0)
            pad = jnp.zeros((SLOT - STEP, HD), F32)
            for tx in range(4):
                piece = jnp.concatenate([chunk[tx * STEP : (tx + 1) * STEP], pad], axis=0)
                out_ref[o, tx, hhi * SLOT : (hhi + 1) * SLOT, :] = piece.astype(BF16)


def row_mask(half, dims, axis):
    def split(value, size):
        whole = jnp.floor((value + 0.5) * (1.0 / size))
        return whole, value - whole * size

    position = lax.broadcasted_iota(jnp.int32, dims, axis).astype(F32)
    group, inside = split(position, BLOCK)
    thi, s = split(group, Z)
    tx, i = split(inside, STEP)
    row = s * (8 * ROWS) + (thi * 4 + tx) * ROWS + (i + (half * HALF).astype(F32))
    return jnp.where((i < HALF - 0.5) & (row < TILE - 0.5), 1.0, 0.0).astype(F32)


def stacked(columns):
    return jnp.concatenate([columns[:, g * HD : (g + 1) * HD].astype(F32).T.astype(BF16) for g in range(4)], axis=0)


def seen_row(ids_ref, count_ref, visible_ref, j):
    y, core, z = ids_ref[0], ids_ref[1], ids_ref[2]
    conv = jnp.where(z < 4, 2 * z, 15 - 2 * z)
    source = ((y - 2 * j) & 3) * 2 + core
    shift = jnp.int32(0)
    for i in range(1, 8):
        shift = jnp.where(source == i, SHIFT[i], shift)
    block = (z + shift) & 7
    seen = jnp.minimum(visible_ref[pl.ds(conv * 8 + block, 1), :], count_ref[conv])
    seen = jnp.where(seen > (y >> 1), 1.0, 0.0).astype(F32)
    return jnp.concatenate([seen] * 4, axis=1)


def weights_of(keys_s, q_t):
    return jnp.exp2(dot(keys_s[...], q_t) * SCALE_LOG2)


def load_pair(ids_ref, mine, other, keys_s, values_s):
    core = ids_ref[1]
    for i in range(2):
        rows = slice(i * MID, (i + 1) * MID)

        @pl.when(core == 0)
        def _():
            keys_s[rows, :] = mine[i][...]
            values_s[rows, :] = other[i][...]

        @pl.when(core != 0)
        def _():
            keys_s[rows, :] = other[i][...]
            values_s[rows, :] = mine[i][...]

    return all_rows(ids_ref, HD, 0)


def all_rows(ids_ref, size, axis):
    half = ids_ref[0] & 1
    dims = (MID, size) if axis == 0 else (size, MID)
    return jnp.concatenate([row_mask(half, dims, axis), row_mask(1 - half, dims, axis)], axis=axis)


def forward(ids_ref, count_ref, visible_ref, mine0, mine1, other0, other1, q0, q1, acc_ref, sums_ref, keys_s, values_s, turned_s):
    ok = load_pair(ids_ref, (mine0, mine1), (other0, other1), keys_s, values_s)
    keys_s[...] = (keys_s[...].astype(F32) * ok).astype(BF16)
    turned_s[0:HD, :] = (values_s[...].astype(F32) * ok).T.astype(BF16)
    turned_s[HD:, :] = all_rows(ids_ref, 16, 1).astype(BF16)
    for j, q in enumerate((q0, q1)):
        q_t = q[0:128, :]
        o_t = q[128:256, :].astype(F32)
        acc = dot(turned_s[...], weights_of(keys_s, q_t).astype(BF16))
        acc = acc * seen_row(ids_ref, count_ref, visible_ref, j)
        both = jnp.concatenate([acc[HD : HD + 1], jnp.sum(acc[:HD] * o_t, axis=0, keepdims=True)], axis=0)
        sums_ref[j] = both
        acc_ref[j] = acc[:HD]


def all_sums(mine_ref, other_ref, j):
    both = mine_ref[j] + other_ref[1 - j]
    total = both[0:1]
    safe = jnp.where(total > 0, total, 1.0)
    return 1.0 / safe, both[1:2] / safe


def backward(
    ids_ref, count_ref, visible_ref, mine0, mine1, other0, other1, q0, q1, acc_ref, s0, s1,
    r0, r1, keep_ref, send_ref, keys_s, values_s, turned_s, dk_s, dv_s,
):
    ok = load_pair(ids_ref, (mine0, mine1), (other0, other1), keys_s, values_s)
    masked = keys_s[...].astype(F32) * ok
    keys_s[...] = masked.astype(BF16)
    turned_s[...] = masked.T.astype(BF16)
    dk_s[...] = jnp.zeros((ALL, HD), F32)
    dv_s[...] = jnp.zeros((ALL, HD), F32)
    for j, (q, r) in enumerate(((q0, r0), (q1, r1))):
        q_t = q[0:128, :]
        o_t = q[128:256, :]
        q_rows = stacked(q_t)
        o_rows = stacked(o_t)
        inverse, delta = all_sums(s0, s1, j)
        acc = (acc_ref[j] * inverse).astype(BF16)
        inverse = inverse * seen_row(ids_ref, count_ref, visible_ref, j)
        prob = weights_of(keys_s, q_t) * inverse
        d_score = (prob * (dot(values_s[...], o_t) - delta)).astype(BF16)
        dk_s[...] += dot(d_score, q_rows)
        dv_s[...] += dot(prob.astype(BF16), o_rows)
        dq = dot(turned_s[...], d_score)
        r[...] = jnp.concatenate([acc, (dq * SCALE).astype(BF16)], axis=0)
    core = ids_ref[1]

    @pl.when(core == 0)
    def _():
        keep_ref[...] = dk_s[...] * (ok * SCALE)
        send_ref[...] = (dv_s[...] * ok).astype(BF16)

    @pl.when(core != 0)
    def _():
        keep_ref[...] = dv_s[...] * ok
        send_ref[...] = (dk_s[...] * (ok * SCALE)).astype(BF16)


def sum_tokens(gate_ref, r0, r1, out_ref):
    gate = gate_value(gate_ref)
    both = r0[...].astype(F32) + r1[...].astype(F32)
    for g in range(4):
        lanes = slice(g * HD, (g + 1) * HD)
        out_ref[0:128, lanes] = (both[0:128, lanes].T * gate).astype(BF16)
        out_ref[128:256, lanes] = both[128:256, lanes].T.astype(BF16)


def norm_back(x, d_normed, gain):
    mean_square = jnp.mean(x * x, axis=-1, keepdims=True)
    inverse = lax.rsqrt(mean_square + EPSILON)
    scaled = d_normed * gain
    dots = jnp.mean(x * scaled, axis=-1, keepdims=True)
    return inverse * scaled - x * (inverse * inverse * inverse * dots)


def finish_queries(queries_ref, got_ref, gain_ref, attended_ref, out_ref):
    gain = gain_ref[...]
    attended_ref[0] = got_ref[0:128, :]
    for g in range(4):
        lanes = slice(g * HD, (g + 1) * HD)
        x = queries_ref[0, :, lanes].astype(F32)
        out_ref[0, :, lanes] = norm_back(x, got_ref[128:256, lanes].astype(F32), gain).astype(BF16)


def finish_keys(keys_ref, got_ref, gain_ref, dk_ref, dv_ref):
    gain = gain_ref[...]
    for n in range(2):
        for head in range(8):
            hhi, hx = divmod(head, 4)
            lanes = slice(head * HD, (head + 1) * HD)
            x = keys_ref[n, :, lanes].astype(F32)

            def rows(kv):
                halves = [got_ref[(n * 2 + half) * 2 + kv, hx, hhi * SLOT : (hhi + 1) * SLOT, :].astype(F32) for half in range(2)]
                return jnp.concatenate([piece[:HALF] for piece in halves], axis=0)

            dk_ref[n, :, lanes] = norm_back(x, rows(0), gain).astype(BF16)
            dv_ref[n, :, lanes] = rows(1).astype(BF16)


def exchange(value, axes):
    return lax.all_to_all(value, axes, split_axis=0, concat_axis=0, tiled=True)


def rotated(value, k):
    return lax.ppermute(value, "y", [(i, (i + k) % Y) for i in range(Y)])


def traded(value):
    return lax.ppermute(value, "y", [(i, i ^ 1) for i in range(Y)])


def swapped(value):
    return lax.ppermute(value, "core", [(0, 1), (1, 0)])


TO_PLANE = [(c * 8 + (z + SHIFT[i]) % 8, i * 8 + z) for i in range(8) for z, c in enumerate(CONV_OF)]
FROM_PLANE = [(b, a) for a, b in TO_PLANE]
PLANES = ("y", "core", "seq")


def shards(queries, keys, values, q_gain, k_gain, gate, tile_count, tile_owner, visible, d_out):
    y, core, z = lax.axis_index("y"), lax.axis_index("core"), lax.axis_index("seq")
    ids = jnp.stack([y, core, z]).astype(jnp.int32)
    q_gain = q_gain.reshape(1, HD)
    k_gain = k_gain.reshape(1, HD)
    seen = visible.reshape(64, 128)

    (packed_kv,) = call(pack_keys, [shape((8, 4, 32, HD), BF16)], keys, values, k_gain)
    packed_kv, queries = lax.optimization_barrier((packed_kv, queries))
    buffers = [pltpu.VMEM((128, 512), BF16), pltpu.VMEM((128, 512), BF16), pltpu.VMEM((1, HD), F32), pltpu.SemaphoreType.DMA((3,))]
    (packed,) = call(
        pack_queries,
        [shape((256, 512), BF16)],
        gate, queries, d_out, q_gain,
        smem=1, hbm=3, scratch=buffers, limit=60 << 20,
    )
    owner = pl.pallas_call(
        owners_of,
        out_shape=shape((N_C,), jnp.int32),
        in_specs=[pl.BlockSpec(memory_space=pltpu.SMEM)] * 2,
        out_specs=pl.BlockSpec(memory_space=pltpu.SMEM),
        cost_estimate=pl.CostEstimate(flops=HEAVY, bytes_accessed=64, transcendentals=0),
        compiler_params=pltpu.CompilerParams(vmem_limit_bytes=1 << 20),
    )(ids, tile_owner)
    (q0,) = call(turn, [shape((256, 512), BF16)], lax.ppermute(packed, PLANES, TO_PLANE), flops=HEAVY)
    got = exchange(packed_kv.reshape(32, 32, HD), ("y", "core", "x"))
    (chosen,) = call(choose_tiles, [shape((2, 8, BLOCK, HD), BF16)], owner, got.reshape(8, 4, 32, HD), smem=1)
    mine = exchange(chosen.reshape(16, BLOCK, HD), ("zhi", "seq")).reshape(MID, HD)
    q1 = rotated(q0, 2)
    mine, q1 = lax.optimization_barrier((mine, q1))
    beside = traded(mine)
    tiles = (mine, beside, swapped(mine), swapped(beside))

    pair = [pltpu.VMEM((ALL, HD), BF16), pltpu.VMEM((ALL, HD), BF16)]
    gradients = [pltpu.VMEM((ALL, HD), F32), pltpu.VMEM((ALL, HD), F32)]
    acc, sums = call(
        forward,
        [shape((BLOCKS, HD, 512), F32), shape((BLOCKS, 2, 512), F32)],
        ids, tile_count, seen, *tiles, q0, q1,
        smem=2, scratch=pair + [pltpu.VMEM((HD + 16, ALL), BF16)], flops=2 * 2 * 1024 * ALL * HD, limit=32 << 20,
    )
    r0, r1, keep, send = call(
        backward,
        [shape((256, 512), BF16)] * 2 + [shape((ALL, HD), F32), shape((ALL, HD), BF16)],
        ids, tile_count, seen, *tiles, q0, q1, acc, sums, rotated(sums, 2),
        smem=2, scratch=pair + [pltpu.VMEM((HD, ALL), BF16)] + gradients, flops=5 * 2 * 1024 * ALL * HD, limit=32 << 20,
    )

    grads = keep + swapped(send).astype(F32)
    grads = (grads[:MID] + traded(grads[MID:].astype(BF16)).astype(F32)).astype(BF16)
    back = exchange(grads.reshape(16, BLOCK, HD), ("zhi", "seq"))
    r1 = rotated(r1, 2)
    (placed,) = call(return_tiles, [shape((8, 4, 32, HD), BF16)], owner, back.reshape(2, 8, BLOCK, HD), smem=1)
    home = exchange(placed.reshape(32, 32, HD), ("y", "core", "x")).reshape(8, 4, 32, HD)
    (summed,) = call(sum_tokens, [shape((256, 512), BF16)], gate, r0, r1, smem=1)
    summed = lax.ppermute(summed, PLANES, FROM_PLANE)
    d_keys, d_values = call(finish_keys, [shape(keys.shape, BF16), shape(values.shape, BF16)], keys, home, k_gain, flops=HEAVY)
    attended, d_queries = call(finish_queries, [shape(queries.shape, BF16)] * 2, queries, summed, q_gain)
    return (attended, d_queries, d_keys, d_values)


def solution(mesh):
    parts = Mesh(mesh.devices.reshape(Y, CORE, Z, 2, 4), ("y", "core", "seq", "zhi", "x"))
    conv, tensor = ("y", "core"), ("zhi", "x")
    tokens = P(conv, "seq", tensor)
    rows = P(conv, ("seq", "zhi", "x"), None)
    in_specs = (tokens, rows, rows, P(), P(), P(), P(), P(), P(), tokens)
    out_specs = (tokens, tokens, rows, rows)
    return jax.shard_map(shards, mesh=parts, in_specs=in_specs, out_specs=out_specs, check_vma=False)
```

```python
import math

import jax
import jax.numpy as jnp
from jax import lax
from jax.experimental import pallas as pl
from jax.experimental.pallas import tpu as pltpu
from jax.sharding import Mesh, PartitionSpec as P

HD = 128
TILE = 1601
ROWS = 26
HALF = 13
SLOT = 16
STEP = 14
EPSILON = 1e-05
SCALE = 1.0 / math.sqrt(HD)
SCALE_LOG2 = SCALE / math.log(2.0)
F32 = jnp.float32
HEAVY = 20_000_000_000
BF16 = jnp.bfloat16

Y, CORE, Z, N_O, N_C = 4, 2, 8, 8, 8
PLANE_OF = (0, 7, 1, 6, 2, 5, 3, 4)
CONV_OF = tuple(PLANE_OF.index(z) for z in range(Z))
SHIFT = (0, 4, 1, 3, 2, 6, 5, 7)
BLOCK = 4 * STEP
MID = 2 * Z * BLOCK


def dot(a, b):
    return jnp.dot(a, b, preferred_element_type=F32)


def call(kernel, outs, *args, smem=0, hbm=0, scratch=(), flops=0, limit=8 << 20):
    specs = [pl.BlockSpec(memory_space=pltpu.SMEM)] * smem
    specs += [pl.BlockSpec(memory_space=pltpu.HBM)] * hbm
    specs += [pl.BlockSpec(memory_space=pltpu.VMEM)] * (len(args) - smem - hbm)
    size = sum(a.size * a.dtype.itemsize for a in args) + sum(o.size * o.dtype.itemsize for o in outs)
    return pl.pallas_call(
        kernel,
        out_shape=outs,
        in_specs=specs,
        out_specs=[pl.BlockSpec(memory_space=pltpu.VMEM)] * len(outs),
        scratch_shapes=list(scratch),
        cost_estimate=pl.CostEstimate(flops=flops, bytes_accessed=size, transcendentals=0),
        compiler_params=pltpu.CompilerParams(vmem_limit_bytes=limit),
    )(*args)


def shape(dims, dtype):
    return jax.ShapeDtypeStruct(dims, dtype)


def gate_value(gate_ref):
    return jnp.tanh(jnp.full((1, HD), gate_ref[0], F32))


def pack_queries(gate_ref, queries_ref, d_out_ref, gain_ref, out_ref, x_s, d_s, gain_s, sems):
    copies = [
        pltpu.make_async_copy(source, target, sems.at[i])
        for i, (source, target) in enumerate(
            ((queries_ref.at[0], x_s), (d_out_ref.at[0], d_s), (gain_ref, gain_s))
        )
    ]
    for copy in copies:
        copy.start()
    gate = gate_value(gate_ref)
    for copy in copies:
        copy.wait()
    gain = gain_s[...]
    for g in range(4):
        lanes = slice(g * HD, (g + 1) * HD)
        x = x_s[:, lanes].astype(F32)
        mean_square = jnp.mean(x * x, axis=-1, keepdims=True)
        out_ref[0:128, lanes] = (x * lax.rsqrt(mean_square + EPSILON) * gain).astype(BF16)
        out_ref[128:256, lanes] = (gate * d_s[:, lanes].astype(F32)).astype(BF16)


def turn(packed_ref, out_ref):
    for g in range(4):
        lanes = slice(g * HD, (g + 1) * HD)
        for rows in (slice(0, 128), slice(128, 256)):
            out_ref[rows, lanes] = packed_ref[rows, lanes].astype(F32).T.astype(BF16)


def pack_keys(keys_ref, values_ref, gain_ref, out_ref):
    gain = gain_ref[...]
    for n in range(2):
        for head in range(8):
            hhi, hx = divmod(head, 4)
            lanes = slice(head * HD, (head + 1) * HD)
            x = keys_ref[n, :, lanes].astype(F32)
            mean_square = jnp.mean(x * x, axis=-1, keepdims=True)
            normed = x * lax.rsqrt(mean_square + EPSILON) * gain
            pad = jnp.zeros((SLOT - HALF, HD), F32)
            for kv, rows in ((0, normed), (1, values_ref[n, :, lanes].astype(F32))):
                for half in range(2):
                    at = (n * 2 + half) * 2 + kv
                    piece = jnp.concatenate([rows[half * HALF : (half + 1) * HALF], pad], axis=0)
                    out_ref[at, hx, hhi * SLOT : (hhi + 1) * SLOT, :] = piece.astype(BF16)


def choose_tiles(owner_ref, got_ref, out_ref):
    for z in range(Z):
        o = jnp.maximum(owner_ref[CONV_OF[z]], 0)
        chunk = got_ref[o].astype(F32)
        for hhi in range(2):
            pieces = [chunk[tx, hhi * SLOT : hhi * SLOT + STEP, :] for tx in range(4)]
            out_ref[hhi, z] = jnp.concatenate(pieces, axis=0).astype(BF16)


def return_tiles(owner_ref, got_ref, out_ref):
    for o in range(N_O):
        found = jnp.int32(-1)
        for c in range(N_C):
            found = jnp.where(owner_ref[c] == o, PLANE_OF[c], found)
        at = jnp.maximum(found, 0)
        for hhi in range(2):
            chunk = jnp.where(found >= 0, got_ref[hhi, at].astype(F32), 0.0)
            pad = jnp.zeros((SLOT - STEP, HD), F32)
            for tx in range(4):
                piece = jnp.concatenate([chunk[tx * STEP : (tx + 1) * STEP], pad], axis=0)
                out_ref[o, tx, hhi * SLOT : (hhi + 1) * SLOT, :] = piece.astype(BF16)


def row_mask(half, dims, axis):
    def split(value, size):
        whole = jnp.floor((value + 0.5) * (1.0 / size))
        return whole, value - whole * size

    position = lax.broadcasted_iota(jnp.int32, dims, axis).astype(F32)
    group, inside = split(position, BLOCK)
    thi, s = split(group, Z)
    tx, i = split(inside, STEP)
    row = s * (8 * ROWS) + (thi * 4 + tx) * ROWS + (i + (half * HALF).astype(F32))
    return jnp.where((i < HALF - 0.5) & (row < TILE - 0.5), 1.0, 0.0).astype(F32)


def stacked(columns):
    return jnp.concatenate([columns[:, g * HD : (g + 1) * HD].astype(F32).T.astype(BF16) for g in range(4)], axis=0)


def seen_row(ids_ref, count_ref, visible_ref, j):
    y, core, z = ids_ref[0], ids_ref[1], ids_ref[2]
    conv = jnp.where(z < 4, 2 * z, 15 - 2 * z)
    source = ((y - j) & 3) * 2 + core
    shift = jnp.int32(0)
    for i in range(1, 8):
        shift = jnp.where(source == i, SHIFT[i], shift)
    block = (z + shift) & 7
    seen = jnp.minimum(visible_ref[pl.ds(conv * 8 + block, 1), :], count_ref[conv])
    seen = jnp.where(seen > (y >> 1), 1.0, 0.0).astype(F32)
    return jnp.concatenate([seen] * 4, axis=1)


def weights_of(keys_s, q_t):
    return jnp.exp2(dot(keys_s[...], q_t) * SCALE_LOG2)


def load_pair(ids_ref, mine_ref, other_ref, keys_s, values_s):
    core = ids_ref[1]

    @pl.when(core == 0)
    def _():
        keys_s[...] = mine_ref[...]
        values_s[...] = other_ref[...]

    @pl.when(core != 0)
    def _():
        keys_s[...] = other_ref[...]
        values_s[...] = mine_ref[...]

    return row_mask(ids_ref[0] & 1, (MID, HD), 0)


def forward(ids_ref, count_ref, visible_ref, mine_ref, other_ref, q0, q1, q2, q3, acc_ref, sums_ref, keys_s, values_s, turned_s, q_s):
    ok = load_pair(ids_ref, mine_ref, other_ref, keys_s, values_s)
    keys_s[...] = (keys_s[...].astype(F32) * ok).astype(BF16)
    turned_s[0:HD, :] = (values_s[...].astype(F32) * ok).T.astype(BF16)
    turned_s[HD:, :] = row_mask(ids_ref[0] & 1, (16, MID), 1).astype(BF16)
    for j, q in enumerate((q0, q1, q2, q3)):
        q_s[j] = q[...]

    def block(j, carry):
        q_t = q_s[j, 0:128, :]
        o_t = q_s[j, 128:256, :].astype(F32)
        acc = dot(turned_s[...], weights_of(keys_s, q_t).astype(BF16))
        acc = acc * seen_row(ids_ref, count_ref, visible_ref, j)
        both = jnp.concatenate([acc[HD : HD + 1], jnp.sum(acc[:HD] * o_t, axis=0, keepdims=True)], axis=0)
        for to in range(Y):
            sums_ref[to, j] = both
        acc_ref[j] = acc[:HD]
        return carry

    lax.fori_loop(0, Y, block, 0, unroll=True)


def all_sums(ids_ref, sums_ref, j):
    y = ids_ref[0]
    both = sums_ref[y, j]
    for k in range(1, Y):
        both = both + sums_ref[(y - k) & 3, (j - k) & 3]
    total = both[0:1]
    safe = jnp.where(total > 0, total, 1.0)
    return 1.0 / safe, both[1:2] / safe


def backward(
    ids_ref, count_ref, visible_ref, mine_ref, other_ref, q0, q1, q2, q3, acc_ref, sums_ref,
    r0, r1, r2, r3, keep_ref, send_ref, keys_s, values_s, turned_s, q_s, dk_s, dv_s,
):
    ok = load_pair(ids_ref, mine_ref, other_ref, keys_s, values_s)
    masked = keys_s[...].astype(F32) * ok
    keys_s[...] = masked.astype(BF16)
    turned_s[...] = masked.T.astype(BF16)
    dk_s[...] = jnp.zeros((MID, HD), F32)
    dv_s[...] = jnp.zeros((MID, HD), F32)
    for j, q in enumerate((q0, q1, q2, q3)):
        q_s[j] = q[...]

    def block(j, carry):
        q_t = q_s[j, 0:128, :]
        o_t = q_s[j, 128:256, :]
        q_rows = stacked(q_t)
        o_rows = stacked(o_t)
        inverse, delta = all_sums(ids_ref, sums_ref, j)
        acc = (acc_ref[j] * inverse).astype(BF16)
        inverse = inverse * seen_row(ids_ref, count_ref, visible_ref, j)
        prob = weights_of(keys_s, q_t) * inverse
        d_score = (prob * (dot(values_s[...], o_t) - delta)).astype(BF16)
        dk_s[...] += dot(d_score, q_rows)
        dv_s[...] += dot(prob.astype(BF16), o_rows)
        dq = dot(turned_s[...], d_score)
        q_s[j] = jnp.concatenate([acc, (dq * SCALE).astype(BF16)], axis=0)
        return carry

    lax.fori_loop(0, Y, block, 0, unroll=2)
    for j, r in enumerate((r0, r1, r2, r3)):
        r[...] = q_s[j]
    core = ids_ref[1]

    @pl.when(core == 0)
    def _():
        keep_ref[...] = dk_s[...] * (ok * SCALE)
        send_ref[...] = (dv_s[...] * ok).astype(BF16)

    @pl.when(core != 0)
    def _():
        keep_ref[...] = dv_s[...] * ok
        send_ref[...] = (dk_s[...] * (ok * SCALE)).astype(BF16)


def sum_tokens(gate_ref, r0, r1, r2, r3, out_ref):
    gate = gate_value(gate_ref)
    both = r0[...].astype(F32) + r1[...].astype(F32) + r2[...].astype(F32) + r3[...].astype(F32)
    for g in range(4):
        lanes = slice(g * HD, (g + 1) * HD)
        out_ref[0:128, lanes] = (both[0:128, lanes].T * gate).astype(BF16)
        out_ref[128:256, lanes] = both[128:256, lanes].T.astype(BF16)


def norm_back(x, d_normed, gain):
    mean_square = jnp.mean(x * x, axis=-1, keepdims=True)
    inverse = lax.rsqrt(mean_square + EPSILON)
    scaled = d_normed * gain
    dots = jnp.mean(x * scaled, axis=-1, keepdims=True)
    return inverse * scaled - x * (inverse * inverse * inverse * dots)


def finish_queries(queries_ref, got_ref, gain_ref, attended_ref, out_ref):
    gain = gain_ref[...]
    attended_ref[0] = got_ref[0:128, :]
    for g in range(4):
        lanes = slice(g * HD, (g + 1) * HD)
        x = queries_ref[0, :, lanes].astype(F32)
        out_ref[0, :, lanes] = norm_back(x, got_ref[128:256, lanes].astype(F32), gain).astype(BF16)


def finish_keys(keys_ref, got_ref, gain_ref, dk_ref, dv_ref):
    gain = gain_ref[...]
    for n in range(2):
        for head in range(8):
            hhi, hx = divmod(head, 4)
            lanes = slice(head * HD, (head + 1) * HD)
            x = keys_ref[n, :, lanes].astype(F32)

            def rows(kv):
                halves = [got_ref[(n * 2 + half) * 2 + kv, hx, hhi * SLOT : (hhi + 1) * SLOT, :].astype(F32) for half in range(2)]
                return jnp.concatenate([piece[:HALF] for piece in halves], axis=0)

            dk_ref[n, :, lanes] = norm_back(x, rows(0), gain).astype(BF16)
            dv_ref[n, :, lanes] = rows(1).astype(BF16)


def exchange(value, axes):
    return lax.all_to_all(value, axes, split_axis=0, concat_axis=0, tiled=True)


def rotated(value, k):
    return lax.ppermute(value, "y", [(i, (i + k) % Y) for i in range(Y)])


def swapped(value):
    return lax.ppermute(value, "core", [(0, 1), (1, 0)])


TO_PLANE = [(c * 8 + (z + SHIFT[i]) % 8, i * 8 + z) for i in range(8) for z, c in enumerate(CONV_OF)]
FROM_PLANE = [(b, a) for a, b in TO_PLANE]
PLANES = ("y", "core", "seq")


def shards(queries, keys, values, q_gain, k_gain, gate, tile_count, tile_owner, visible, d_out):
    y, core, z = lax.axis_index("y"), lax.axis_index("core"), lax.axis_index("seq")
    ids = jnp.stack([y, core, z]).astype(jnp.int32)
    q_gain = q_gain.reshape(1, HD)
    k_gain = k_gain.reshape(1, HD)
    owner = lax.dynamic_index_in_dim(tile_owner, y // 2, 1, keepdims=False)
    seen = visible.reshape(64, 128)

    buffers = [pltpu.VMEM((128, 512), BF16), pltpu.VMEM((128, 512), BF16), pltpu.VMEM((1, HD), F32), pltpu.SemaphoreType.DMA((3,))]
    (packed,) = call(
        pack_queries,
        [shape((256, 512), BF16)],
        gate, queries, d_out, q_gain,
        smem=1, hbm=3, scratch=buffers, limit=60 << 20,
    )
    packed, k_gain = lax.optimization_barrier((packed, k_gain))
    (q0,) = call(turn, [shape((256, 512), BF16)], lax.ppermute(packed, PLANES, TO_PLANE), flops=HEAVY)
    (packed_kv,) = call(pack_keys, [shape((8, 4, 32, HD), BF16)], keys, values, k_gain)
    got = exchange(packed_kv.reshape(32, 32, HD), ("y", "core", "x"))
    (chosen,) = call(choose_tiles, [shape((2, 8, BLOCK, HD), BF16)], owner, got.reshape(8, 4, 32, HD), smem=1)
    mine = exchange(chosen.reshape(16, BLOCK, HD), ("zhi", "seq")).reshape(MID, HD)
    q1, q2, q3 = rotated(q0, 1), rotated(q0, 2), rotated(q0, 3)
    other = swapped(mine)

    pair = [pltpu.VMEM((MID, HD), BF16), pltpu.VMEM((MID, HD), BF16)]
    tokens = pltpu.VMEM((Y, 256, 512), BF16)
    gradients = [pltpu.VMEM((MID, HD), F32), pltpu.VMEM((MID, HD), F32)]
    acc, sums = call(
        forward,
        [shape((Y, HD, 512), F32), shape((Y, Y, 2, 512), F32)],
        ids, tile_count, seen, mine, other, q0, q1, q2, q3,
        smem=2, scratch=pair + [pltpu.VMEM((HD + 16, MID), BF16), tokens], flops=2 * 2 * 2048 * MID * HD, limit=32 << 20,
    )
    sums = exchange(sums, "y")
    r0, r1, r2, r3, keep, send = call(
        backward,
        [shape((256, 512), BF16)] * 4 + [shape((MID, HD), F32), shape((MID, HD), BF16)],
        ids, tile_count, seen, mine, other, q0, q1, q2, q3, acc, sums,
        smem=2, scratch=pair + [pltpu.VMEM((HD, MID), BF16), tokens] + gradients, flops=5 * 2 * 2048 * MID * HD, limit=32 << 20,
    )

    grads = (keep + swapped(send).astype(F32)).astype(BF16)
    back = exchange(grads.reshape(16, BLOCK, HD), ("zhi", "seq"))
    r1, r2, r3 = rotated(r1, 3), rotated(r2, 2), rotated(r3, 1)
    (placed,) = call(return_tiles, [shape((8, 4, 32, HD), BF16)], owner, back.reshape(2, 8, BLOCK, HD), smem=1)
    home = exchange(placed.reshape(32, 32, HD), ("y", "core", "x")).reshape(8, 4, 32, HD)
    r1, r2, r3, placed = lax.optimization_barrier((r1, r2, r3, placed))
    (summed,) = call(sum_tokens, [shape((256, 512), BF16)], gate, r0, r1, r2, r3, smem=1)
    summed = lax.ppermute(summed, PLANES, FROM_PLANE)
    d_keys, d_values = call(finish_keys, [shape(keys.shape, BF16), shape(values.shape, BF16)], keys, home, k_gain, flops=HEAVY)
    attended, d_queries = call(finish_queries, [shape(queries.shape, BF16)] * 2, queries, summed, q_gain)
    return (attended, d_queries, d_keys, d_values)


def solution(mesh):
    parts = Mesh(mesh.devices.reshape(Y, CORE, Z, 2, 4), ("y", "core", "seq", "zhi", "x"))
    conv, tensor = ("y", "core"), ("zhi", "x")
    tokens = P(conv, "seq", tensor)
    rows = P(conv, ("seq", "zhi", "x"), None)
    in_specs = (tokens, rows, rows, P(), P(), P(), P(), P(), P(), tokens)
    out_specs = (tokens, tokens, rows, rows)
    return jax.shard_map(shards, mesh=parts, in_specs=in_specs, out_specs=out_specs, check_vma=False)
```
